128 devices in a mesh: pipe: 4 (over x), expert: 32 (over z, y, core).
Axes of the slice: x: 4, y: 4, z: 4, core: 2. Of those that a mesh axis runs over, the one named last changes fastest.
Arguments:
- inputs: bfloat16 [4, 1024, 3584], P(None, 'expert'), may hold values from -6 to 6
- cotangent: bfloat16 [4, 1024, 3584], P(None, 'expert'), may hold values from -6 to 6
- norm_gain: float32 [4, 3584], P('pipe'), may hold values from 0.5 to 1.5
- router_weight: bfloat16 [4, 3584, 16], P('pipe'), may hold values from -0.09375 to 0.09375
- gate_weight: bfloat16 [4, 3584, 16384], P('pipe', None, 'expert'), may hold values from -0.09375 to 0.09375
- up_weight: bfloat16 [4, 3584, 16384], P('pipe', None, 'expert'), may hold values from -0.09375 to 0.09375
- down_weight: bfloat16 [4, 16384, 3584], P('pipe', 'expert'), may hold values from -0.1875 to 0.1875
- route_ids: int32 [4, 4, 1024, 2], P('pipe', None, 'expert'), may hold values from 0 to 15, all different within a row; in each aligned block of 32 rows (0 to 31, 32 to 63, ..., all dimensions but the last counted through in order) at most 5 rows name the same one
Outputs:
- activations: bfloat16 [4, 4, 1024, 3584], P('pipe', None, 'expert')
- input_grads: bfloat16 [4, 4, 1024, 3584], P('pipe', None, 'expert')
The draws below stay inside these ranges and needn't reach their ends.
Inputs may be any that keep to these rules, and one draw needn't show every extreme that they name: `route_ids`: in each aligned block of 32 rows (one device's tokens of one micro-batch at one section) every token names 2 different experts, no expert is named by more than 5 rows, and in some blocks an expert is named by exactly 5 rows.
All inputs are finite; a program needn't handle non-finite values.
Results may differ from the reference program's by a relative error of at most 0.03.
Values may be sent and summed in bfloat16 or wider, within the bound.
A program may use at most 128 MiB of HBM per device.

```python
import math
import jax
import jax.numpy as jnp
import numpy as np
from jax import lax

D = 3584
HID = 1024
TOPK = 2
MICRO = 4
TOK_DEV = 32
SECTIONS = 4
EXPERTS = 16
TOKENS = 1024
CAP = 5
N_EXPERT = 32


def shard_levels(key, dims, pieces, least, top_value):
    level = 1.0
    for axis_at, blocks in pieces:
        draws = jax.random.uniform(jax.random.fold_in(jax.random.fold_in(key, 6), axis_at), (blocks,), jnp.float32, least / len(pieces), top_value / len(pieces))
        level = level * jnp.repeat(jnp.exp(draws), dims[axis_at] // blocks).reshape((-1,) + (1,) * (len(dims) - 1 - axis_at))
    return level


def assign_block(own_key, own, number, rows, count, top, most, lean):
    sequence = jax.random.permutation(own_key, count)
    crowded, usual = portions_of(count, rows * top, most, lean, True), portions_of(count, rows * top, most, lean, False)
    places = jnp.arange(count)

    def named(lengths, turn):
        used = int((lengths > 0).sum())
        fixed = max(1, used // 4)
        passed = fixed + (places - fixed + turn * (used - fixed)) % max(1, count - fixed)
        return jnp.zeros((count,), jnp.int32).at[sequence[jnp.where(places < fixed, places, passed)]].set(jnp.asarray(lengths, jnp.int32))

    lengths = jnp.where(number % 4 == 0, named(crowded, number // 4), named(usual, number - number // 4 - 1))
    mixed = jax.random.permutation(jax.random.fold_in(own, 3), count)
    donor, receiver = mixed[0:count // 2 * 2:2], mixed[1:count // 2 * 2:2]
    margin = jnp.minimum(lengths[donor] - 1, most - lengths[receiver]) // 2
    margin = jnp.where((donor == sequence[0]) | (receiver == sequence[0]) | (lengths[receiver] == 0), 0, jnp.maximum(margin, 0))
    passed = jax.random.randint(jax.random.fold_in(own, 4), (count // 2,), 0, 1 << 20) % (margin + 1)
    lengths = lengths.at[donor].add(-passed).at[receiver].add(passed)
    items = jnp.searchsorted(jnp.cumsum(lengths), jnp.arange(rows * top), side="right").astype(jnp.int32)
    table = items.reshape(top, rows).T
    table = table[jax.random.permutation(jax.random.fold_in(own, 1), rows)]
    turn = jax.random.randint(jax.random.fold_in(own, 2), (rows, 1), 0, top)
    return jnp.take_along_axis(table, (jnp.arange(top)[None, :] + turn) % top, axis=1)


def portions_of(amount, total, reach, lean, full):
    portions = [(1 << 20) // math.isqrt(rank ** lean) + 1 for rank in range(1, amount + 1)]
    largest = reach if full else min(reach, max(-(-total // amount), total * portions[0] // sum(portions)))
    least = 1 if total - largest >= amount - 1 else 0
    counts, surplus = [largest] + [least] * (amount - 1), total - largest - least * (amount - 1)
    while surplus > 0:
        free = [i for i in range(1, amount) if counts[i] < largest] or [i for i in range(1, amount) if counts[i] < reach]
        pool, left = sum([portions[i] for i in free]), surplus
        for i in free:
            addition = min(reach - counts[i], max(1, left * portions[i] // pool), surplus)
            counts[i] = counts[i] + addition
            surplus = surplus - addition
    return np.array(counts)


def gaussian(rng, extent, spread, limit, cuts=(), kind=jnp.bfloat16):
    array = spread * jax.random.normal(rng, extent, jnp.float32)
    if cuts:
        array = array * shard_levels(rng, extent, cuts, -0.22, 0.18)
    return jnp.clip(array, -limit, limit).astype(kind)


def setup_inputs(seed: int = 0) -> dict:
    seeds = jax.random.split(jax.random.key(seed), 9)
    inputs = gaussian(seeds[0], (MICRO, TOKENS, D), 1.0, 6.0, ((1, 32),))
    cotangent = gaussian(seeds[1], (MICRO, TOKENS, D), 1.0, 6.0, ((1, 32),))
    norm_gain = jnp.clip(1.0 + 0.1 * jax.random.normal(seeds[2], (SECTIONS, D), jnp.float32), 0.5, 1.5)
    router_weight = gaussian(seeds[3], (SECTIONS, D, EXPERTS), D ** -0.5, 0.09375, ((0, 4),))
    gate_weight = gaussian(seeds[4], (SECTIONS, D, EXPERTS * HID), D ** -0.5, 0.09375, ((0, 4), (2, 32)))
    up_weight = gaussian(seeds[5], (SECTIONS, D, EXPERTS * HID), D ** -0.5, 0.09375, ((0, 4), (2, 32)))
    down_weight = gaussian(seeds[6], (SECTIONS, EXPERTS * HID, D), HID ** -0.5, 0.1875, ((0, 4), (1, 32)))
    route_ids_keys = jax.random.split(jax.random.fold_in(seeds[7], 1), SECTIONS * MICRO * TOKENS // TOK_DEV)
    route_ids_turns = jax.random.permutation(jax.random.fold_in(seeds[7], 3), SECTIONS * MICRO * TOKENS // TOK_DEV)
    route_ids = jax.vmap(lambda own, number: assign_block(jax.random.fold_in(seeds[7], 2), own, number, TOK_DEV, EXPERTS, TOPK, CAP, 2))(route_ids_keys, route_ids_turns).reshape((SECTIONS, MICRO, TOKENS, TOPK))
    return {"inputs": inputs, "cotangent": cotangent, "norm_gain": norm_gain, "router_weight": router_weight, "gate_weight": gate_weight, "up_weight": up_weight, "down_weight": down_weight, "route_ids": route_ids}


EPSILON = 1e-06

def settle(values):
    return lax.optimization_barrier(values)

def half_weights(w_gate, w_up, w_down, expert, half_index):
    column_start = expert * HID + half_index * (HID // 2)
    return (lax.dynamic_slice_in_dim(w_gate, column_start, HID // 2, axis=1), lax.dynamic_slice_in_dim(w_up, column_start, HID // 2, axis=1), lax.dynamic_slice_in_dim(w_down, column_start, HID // 2, axis=0))

def expert_rows(flat_ids, expert):
    rows_cap = N_EXPERT * CAP
    chosen = (flat_ids == expert).astype(jnp.int32)
    position = (jnp.cumsum(chosen) - 1).astype(jnp.int32)
    target = jnp.where(chosen > 0, position, rows_cap).astype(jnp.int32)
    pair_count = flat_ids.shape[0]
    pair_of_row = jnp.zeros((rows_cap + 1,), jnp.int32).at[target].set(jnp.arange(pair_count, dtype=jnp.int32))[:rows_cap]
    live_row = jnp.zeros((rows_cap + 1,), jnp.int32).at[target].set(jnp.ones((pair_count,), jnp.int32))[:rows_cap]
    slot_of_pair = jnp.clip(position, 0, rows_cap - 1).astype(jnp.int32)
    return (chosen, pair_of_row, live_row, slot_of_pair)

def moe_forward(normed, expert_ids, w_gate, w_up, w_down):
    flat_ids = expert_ids.reshape(-1)
    pair_count = flat_ids.shape[0]

    def visit(running, expert):
        chosen, pair_of_row, live_row, slot_of_pair = expert_rows(flat_ids, expert)
        gathered = normed[pair_of_row // TOPK]
        rows_in = jnp.where(live_row[:, None] > 0, gathered, jnp.zeros_like(gathered))
        summed = jnp.zeros((rows_in.shape[0], D), jnp.float32)
        for half_index in range(2):
            w_g, w_u, w_d = half_weights(w_gate, w_up, w_down, expert, half_index)
            gate_pre = jnp.dot(rows_in, w_g, preferred_element_type=jnp.float32)
            up_pre = jnp.dot(rows_in, w_u, preferred_element_type=jnp.float32)
            hidden = (jax.nn.silu(gate_pre) * up_pre).astype(jnp.bfloat16)
            partial_value = settle(jnp.dot(hidden, w_d, preferred_element_type=jnp.float32).astype(jnp.bfloat16))
            summed = summed + partial_value.astype(jnp.float32)
        out_rows = settle(summed.astype(jnp.bfloat16)).astype(jnp.float32)
        contrib = jnp.where(chosen[:, None] > 0, out_rows[slot_of_pair], jnp.zeros((pair_count, D), jnp.float32))
        return (running + contrib, None)
    picked, unused = lax.scan(visit, jnp.zeros((pair_count, D), jnp.float32), jnp.arange(EXPERTS, dtype=jnp.int32))
    return picked

def moe_backward(normed, expert_ids, scaled, w_gate, w_up, w_down):
    flat_ids = expert_ids.reshape(-1)
    pair_count = flat_ids.shape[0]

    def visit(running, expert):
        chosen, pair_of_row, live_row, slot_of_pair = expert_rows(flat_ids, expert)
        gathered = normed[pair_of_row // TOPK]
        rows_in = jnp.where(live_row[:, None] > 0, gathered, jnp.zeros_like(gathered))
        grad_taken = scaled[pair_of_row]
        rows_grad = jnp.where(live_row[:, None] > 0, grad_taken, jnp.zeros_like(grad_taken))
        summed = jnp.zeros((rows_in.shape[0], D), jnp.float32)
        for half_index in range(2):
            w_g, w_u, w_d = half_weights(w_gate, w_up, w_down, expert, half_index)
            gate_pre = jnp.dot(rows_in, w_g, preferred_element_type=jnp.float32)
            up_pre = jnp.dot(rows_in, w_u, preferred_element_type=jnp.float32)
            hidden_grad = jnp.dot(rows_grad, w_d.T, preferred_element_type=jnp.float32)
            sigmoid_gate = jax.nn.sigmoid(gate_pre)
            pre_grad = (hidden_grad * up_pre * sigmoid_gate * (1.0 + gate_pre * (1.0 - sigmoid_gate))).astype(jnp.bfloat16)
            up_grad = (hidden_grad * gate_pre * sigmoid_gate).astype(jnp.bfloat16)
            back_part = jnp.dot(pre_grad, w_g.T, preferred_element_type=jnp.float32) + jnp.dot(up_grad, w_u.T, preferred_element_type=jnp.float32)
            back_part = settle(back_part.astype(jnp.bfloat16))
            summed = summed + back_part.astype(jnp.float32)
        out_rows = settle(summed.astype(jnp.bfloat16)).astype(jnp.float32)
        contrib = jnp.where(chosen[:, None] > 0, out_rows[slot_of_pair], jnp.zeros((pair_count, D), jnp.float32))
        return (running + contrib, None)
    pair_grad, unused = lax.scan(visit, jnp.zeros((pair_count, D), jnp.float32), jnp.arange(EXPERTS, dtype=jnp.int32))
    return pair_grad

def section_forward(layer_input, norm_scale, router, w_gate, w_up, w_down, expert_ids):
    input_wide = layer_input.astype(jnp.float32)
    scale_rows = lax.rsqrt(lax.optimization_barrier(jnp.mean(input_wide * input_wide, axis=1, keepdims=True)) + EPSILON)
    normed = (input_wide * scale_rows * norm_scale[None, :]).astype(jnp.bfloat16)
    logits = jnp.dot(normed, router, preferred_element_type=jnp.float32)
    one_hot = (expert_ids[:, :, None] == jnp.arange(EXPERTS, dtype=jnp.int32)[None, None, :]).astype(jnp.float32)
    scores = lax.optimization_barrier(jnp.sum(logits[:, None, :] * one_hot, axis=2))
    probabilities = jax.nn.sigmoid(scores)
    totals = lax.optimization_barrier(jnp.sum(probabilities, axis=1, keepdims=True))
    gate_values = probabilities / totals
    picked = moe_forward(normed, expert_ids, w_gate, w_up, w_down).reshape(TOKENS, TOPK, D)
    layer_output = (input_wide + lax.optimization_barrier(jnp.sum(gate_values[:, :, None] * picked, axis=1))).astype(jnp.bfloat16)
    return (layer_output, (input_wide, scale_rows, normed, one_hot, probabilities, totals, gate_values, picked))

def section_backward(grad_out, saved, norm_scale, router, w_gate, w_up, w_down, expert_ids):
    input_wide, scale_rows, normed, one_hot, probabilities, totals, gate_values, picked = saved
    grad_wide = grad_out.astype(jnp.float32)
    gate_grad = jnp.einsum('tkd,td->tk', picked, grad_wide, precision=lax.Precision.HIGHEST)
    weighted = lax.optimization_barrier(jnp.sum(gate_values * gate_grad, axis=1, keepdims=True))
    score_grad = (gate_grad - weighted) / totals * probabilities * (1.0 - probabilities)
    router_table = lax.optimization_barrier(jnp.sum(score_grad[:, :, None] * one_hot, axis=1)).astype(jnp.bfloat16)
    router_part = jnp.dot(router_table, router.T, preferred_element_type=jnp.float32)
    scaled = (gate_values[:, :, None] * grad_wide[:, None, :]).astype(jnp.bfloat16).reshape(TOKENS * TOPK, D)
    pair_grad = moe_backward(normed, expert_ids, scaled, w_gate, w_up, w_down)
    expert_part = lax.optimization_barrier(jnp.sum(pair_grad.reshape(TOKENS, TOPK, D), axis=1))
    normed_grad = (expert_part + router_part) * norm_scale[None, :]
    inner_term = lax.optimization_barrier(jnp.mean(input_wide * normed_grad, axis=1, keepdims=True))
    result = grad_wide + scale_rows * normed_grad - input_wide * scale_rows ** 3 * inner_term
    return result.astype(jnp.bfloat16)

def reference(inputs, cotangent, norm_gain, router_weight, gate_weight, up_weight, down_weight, route_ids):
    forward_lists = [[] for section_number in range(SECTIONS)]
    backward_lists = [[] for section_number in range(SECTIONS)]
    for micro_index in range(MICRO):
        layer_input = inputs[micro_index]
        kept_states = []
        for section_number in range(SECTIONS):
            layer_input, saved = section_forward(layer_input, norm_gain[section_number], router_weight[section_number], gate_weight[section_number], up_weight[section_number], down_weight[section_number], route_ids[section_number, micro_index])
            kept_states.append(saved)
            forward_lists[section_number].append(layer_input)
        grad_out = cotangent[micro_index]
        for section_number in reversed(range(SECTIONS)):
            grad_out = section_backward(grad_out, kept_states[section_number], norm_gain[section_number], router_weight[section_number], gate_weight[section_number], up_weight[section_number], down_weight[section_number], route_ids[section_number, micro_index])
            backward_lists[section_number].append(grad_out)
    activations = jnp.stack([jnp.stack(entries) for entries in forward_lists])
    input_grads = jnp.stack([jnp.stack(entries) for entries in backward_lists])
    return (activations, input_grads)
```

```python
import functools
import math

import jax
import jax.numpy as jnp
from jax import lax
from jax.experimental import pallas as pl
from jax.experimental.pallas import tpu as pltpu
from jax.sharding import PartitionSpec as P

EPSILON = 1e-06
PIECES = 4
MESH = pl.DeviceIdType.MESH


def grid_of(chips):
    rows = math.isqrt(chips)
    while chips % rows:
        rows -= 1
    return rows, chips // rows


def block_rows(capacity):
    return -(-PIECES * capacity // 8) * 8


def matmul(left, right):
    return jnp.dot(left, right, preferred_element_type=jnp.float32)


def matmul_t(left, right):
    return lax.dot_general(
        left, right, (((1,), (1,)), ((), ())), preferred_element_type=jnp.float32
    )


def relay_kernel(
    geometry,
    inputs_ref,
    cotangent_ref,
    gain_ref,
    router_ref,
    wg_hbm,
    wu_hbm,
    wd_hbm,
    row_table_ref,
    col_table_ref,
    ids_ref,
    out_ref,
    grad_ref,
    wg,
    wu,
    wd,
    acts,
    grads,
    unpack,
    repack,
    dispatch_send,
    dispatch_recv,
    partner_rows,
    combine_send,
    combine_recv,
    half_send,
    half_own,
    half_recv,
    rows_in,
    gate_saved,
    up_saved,
    picked,
    stats,
    weight_sem,
    act_sem,
    grad_sem,
    pipe_sem,
    dispatch_send_sem,
    dispatch_recv_sem,
    swap_send_sem,
    swap_recv_sem,
    half_send_sem,
    half_recv_sem,
    combine_send_sem,
    combine_recv_sem,
):
    sections, micro_count, chips, capacity, offsets, slots = geometry
    lines, columns = grid_of(chips)
    block = block_rows(capacity)
    tokens, width = acts.shape[1], acts.shape[2]
    piece = width // PIECES
    group = chips * capacity
    hidden = wg.shape[1]
    experts = router_ref.shape[1]
    section = lax.axis_index("pipe")
    place = lax.axis_index("expert")
    core = lax.rem(place, 2)
    chip = place // 2
    line, column = chip // columns, lax.rem(chip, columns)
    partner = chip * 2 + (1 - core)
    others = pl.ds(1, chips - 1)

    def peer(step, sign):
        to_line = lax.rem(line + sign * (step // columns) + lines, lines)
        to_column = lax.rem(column + sign * lax.rem(step, columns) + columns, columns)
        return {"expert": (to_line * columns + to_column) * 2 + core}

    def pieces_of(value):
        return [value[:, q * piece : (q + 1) * piece] for q in range(PIECES)]

    barrier = pltpu.get_barrier_semaphore()

    def greet(step, carry):
        pl.semaphore_signal(barrier, inc=1, device_id=peer(step, 1), device_id_type=MESH)
        return carry

    weights = [
        pltpu.make_async_copy(source, target, weight_sem.at[i])
        for i, (source, target) in enumerate([(wg_hbm, wg), (wu_hbm, wu), (wd_hbm, wd)])
    ]

    @pl.when(section == 0)
    def _():
        for m in range(micro_count):
            pltpu.make_async_copy(inputs_ref.at[m], acts.at[m], act_sem.at[m]).start()

    @pl.when(section == sections - 1)
    def _():
        for m in range(micro_count):
            pltpu.make_async_copy(cotangent_ref.at[m], grads.at[m], grad_sem.at[m]).start()

    for copy in weights:
        copy.start()
    lax.fori_loop(1, chips, greet, 0)
    pl.semaphore_signal(barrier, inc=1, device_id={"expert": partner}, device_id_type=MESH)
    for sign in (1, sections - 1):
        pl.semaphore_signal(
            barrier,
            inc=1,
            device_id={"pipe": lax.rem(section + sign, sections)},
            device_id_type=MESH,
        )

    def place_of(number):
        within = lax.rem(number, block)
        q = within // capacity
        row = q * group + (number // block) * capacity + lax.rem(within, capacity)
        return jnp.where(within < PIECES * capacity, row, -1)

    wide = lax.broadcasted_iota(jnp.int32, (PIECES * group, chips * block), 1)
    tall = lax.broadcasted_iota(jnp.int32, (PIECES * group, chips * block), 0)
    unpack[...] = jnp.where(place_of(wide) == tall, 1.0, 0.0).astype(jnp.bfloat16)
    tall = lax.broadcasted_iota(jnp.int32, (chips * block, PIECES * group), 0)
    wide = lax.broadcasted_iota(jnp.int32, (chips * block, PIECES * group), 1)
    repack[...] = jnp.where(place_of(tall) == wide, 1.0, 0.0).astype(jnp.bfloat16)

    pl.semaphore_wait(barrier, chips - 1 + 1 + 2)

    def wait_all(buffer, semaphore):
        pltpu.make_async_copy(buffer, buffer, semaphore).wait()

    def send_blocks(send, recv, send_sem, recv_sem, sign):
        def start(step, carry):
            pltpu.make_async_remote_copy(
                src_ref=send.at[step],
                dst_ref=recv.at[step],
                send_sem=send_sem,
                recv_sem=recv_sem,
                device_id=peer(step, sign),
                device_id_type=MESH,
            ).start()
            return carry

        lax.fori_loop(1, chips, start, 0)

    def post(values, send, recv, send_sem, recv_sem, sign):
        values = values.astype(jnp.bfloat16).reshape(chips, block, piece)
        recv[0] = values[0]
        send[others] = values[1:]
        send_blocks(send, recv, send_sem, recv_sem, sign)

    def table_rows(m):
        lanes = PIECES * tokens
        rows = lax.broadcasted_iota(jnp.int32, (chips * block, 2 * lanes), 0)
        return jnp.where(rows == row_table_ref[m], 1.0, 0.0).astype(jnp.bfloat16)

    def table_columns(m):
        places = lax.broadcasted_iota(jnp.int32, (2 * PIECES * tokens, chips * block), 1)
        return jnp.where(places == col_table_ref[m], 1.0, 0.0).astype(jnp.bfloat16)

    def expert_hot(m, k):
        names = lax.broadcasted_iota(jnp.int32, (tokens, experts), 1)
        return jnp.where(names == ids_ref[m, k], 1.0, 0.0)

    def swap_and_unpack(m, way):
        slot = 2 * way + lax.rem(m, 2)
        wait_all(dispatch_recv.at[m, others], dispatch_recv_sem.at[m])
        swap = pltpu.make_async_remote_copy(
            src_ref=dispatch_recv.at[m],
            dst_ref=partner_rows.at[m],
            send_sem=swap_send_sem,
            recv_sem=swap_recv_sem.at[m],
            device_id={"expert": partner},
            device_id_type=MESH,
        )
        swap.start()
        wait_all(dispatch_send.at[slot, others], dispatch_send_sem.at[slot])
        for part, source in enumerate((dispatch_recv, partner_rows)):
            if part == 1:
                swap.wait()
            flat = source[m].reshape(chips * block, piece)
            rows = matmul(unpack[...], flat).astype(jnp.bfloat16)
            for q in range(PIECES):
                rows_in[q, part * group : (part + 1) * group] = rows[q * group : (q + 1) * group]

    def halves_and_combine(m, way, product):
        slot = 2 * way + lax.rem(m, 2)

        def half_copy(q):
            return pltpu.make_async_remote_copy(
                src_ref=half_send.at[q],
                dst_ref=half_recv.at[m, q],
                send_sem=half_send_sem,
                recv_sem=half_recv_sem.at[m],
                device_id={"expert": partner},
                device_id_type=MESH,
            )

        for q in range(PIECES):
            part = product(q).astype(jnp.bfloat16)
            half_own[q] = part[:group]
            half_send[q] = part[group:]
            half_copy(q).start()
        wait_all(half_recv.at[m], half_recv_sem.at[m])
        total = half_own[...].astype(jnp.float32) + half_recv[m].astype(jnp.float32)
        total = total.astype(jnp.bfloat16).reshape(PIECES * group, piece)
        post(
            matmul(repack[...], total),
            combine_send.at[slot],
            combine_recv.at[m],
            combine_send_sem.at[slot],
            combine_recv_sem.at[m],
            -1,
        )
        wait_all(half_send, half_send_sem)

    def forward_send(m):
        wait_all(acts.at[m], act_sem.at[m])
        wide_in = acts[m].astype(jnp.float32)
        scale = lax.rsqrt(jnp.mean(wide_in * wide_in, axis=1, keepdims=True) + EPSILON)
        normed = (wide_in * scale * gain_ref[...]).astype(jnp.bfloat16)
        stacked = jnp.concatenate(pieces_of(normed), axis=0)
        table = table_rows(m)
        lanes = PIECES * tokens
        slot = lax.rem(m, 2)
        post(
            matmul(table[:, :lanes] + table[:, lanes:], stacked),
            dispatch_send.at[slot],
            dispatch_recv.at[m],
            dispatch_send_sem.at[slot],
            dispatch_recv_sem.at[m],
            1,
        )
        logits = matmul(normed, router_ref[...])
        chances = []
        for k in range(2):
            score = jnp.sum(logits * expert_hot(m, k), axis=1, keepdims=True)
            chances.append(1.0 / (1.0 + jnp.exp(-score)))
        total = chances[0] + chances[1]
        stats[m, 0] = scale
        stats[m, 1] = chances[0]
        stats[m, 2] = chances[1]
        stats[m, 3] = chances[0] / total
        stats[m, 4] = chances[1] / total

    def forward_expert(m):
        swap_and_unpack(m, 0)
        gate_pre = jnp.zeros((2 * group, hidden), jnp.float32)
        up_pre = jnp.zeros((2 * group, hidden), jnp.float32)
        for q in range(PIECES):
            span = slice(q * piece, (q + 1) * piece)
            gate_pre += matmul(rows_in[q], wg[span])
            up_pre += matmul(rows_in[q], wu[span])
        gate_saved[m] = gate_pre
        up_saved[m] = up_pre
        inner = (gate_pre / (1.0 + jnp.exp(-gate_pre)) * up_pre).astype(jnp.bfloat16)
        halves_and_combine(
            m, 0, lambda q: matmul(inner, wd[:, q * piece : (q + 1) * piece])
        )

    def forward_finish(m):
        wait_all(combine_recv.at[m, others], combine_recv_sem.at[m])
        slot = lax.rem(m, 2)
        wait_all(combine_send.at[slot, others], combine_send_sem.at[slot])
        found = matmul(table_columns(m), combine_recv[m].reshape(chips * block, piece))
        for q in range(PIECES):
            span = slice(q * piece, (q + 1) * piece)
            total = acts[m, :, span].astype(jnp.float32)
            for k in range(2):
                begin = (k * PIECES + q) * tokens
                rows = found[begin : begin + tokens]
                picked[m, k, :, span] = rows.astype(jnp.bfloat16)
                total += stats[m, 3 + k] * rows
            out_ref[m, :, span] = total.astype(jnp.bfloat16)

        @pl.when(section < sections - 1)
        def _():
            pltpu.make_async_remote_copy(
                src_ref=out_ref.at[m],
                dst_ref=acts.at[m],
                send_sem=pipe_sem.at[0],
                recv_sem=act_sem.at[m],
                device_id={"pipe": section + 1},
                device_id_type=MESH,
            ).start()

    def backward_send(m):
        wait_all(grads.at[m], grad_sem.at[m])
        upstream = grads[m].astype(jnp.float32)
        stacked = []
        for k in range(2):
            stacked += pieces_of((stats[m, 3 + k] * upstream).astype(jnp.bfloat16))
        slot = 2 + lax.rem(m, 2)
        post(
            matmul(table_rows(m), jnp.concatenate(stacked, axis=0)),
            dispatch_send.at[slot],
            dispatch_recv.at[m],
            dispatch_send_sem.at[slot],
            dispatch_recv_sem.at[m],
            1,
        )
        slopes = [
            jnp.sum(upstream * picked[m, k].astype(jnp.float32), axis=1, keepdims=True)
            for k in range(2)
        ]
        weighted = stats[m, 3] * slopes[0] + stats[m, 4] * slopes[1]
        total = stats[m, 1] + stats[m, 2]
        for k in range(2):
            chance = stats[m, 1 + k]
            stats[m, 5 + k] = (slopes[k] - weighted) / total * chance * (1.0 - chance)

    def backward_expert(m):
        swap_and_unpack(m, 1)
        hidden_grad = jnp.zeros((2 * group, hidden), jnp.float32)
        for q in range(PIECES):
            hidden_grad += matmul_t(rows_in[q], wd[:, q * piece : (q + 1) * piece])
        gate_pre = gate_saved[m]
        sigmoid = 1.0 / (1.0 + jnp.exp(-gate_pre))
        pre_grad = (
            hidden_grad * up_saved[m] * sigmoid * (1.0 + gate_pre * (1.0 - sigmoid))
        ).astype(jnp.bfloat16)
        up_grad = (hidden_grad * gate_pre * sigmoid).astype(jnp.bfloat16)

        def product(q):
            span = slice(q * piece, (q + 1) * piece)
            return matmul_t(pre_grad, wg[span]) + matmul_t(up_grad, wu[span])

        halves_and_combine(m, 1, product)

    def backward_finish(m):
        wait_all(combine_recv.at[m, others], combine_recv_sem.at[m])
        slot = 2 + lax.rem(m, 2)
        wait_all(combine_send.at[slot, others], combine_send_sem.at[slot])
        table = table_columns(m)
        lanes = PIECES * tokens
        summed = matmul(
            table[:lanes] + table[lanes:], combine_recv[m].reshape(chips * block, piece)
        )
        router_table = (
            stats[m, 5] * expert_hot(m, 0) + stats[m, 6] * expert_hot(m, 1)
        ).astype(jnp.bfloat16)
        scale = stats[m, 0]
        inner = jnp.zeros((tokens, 1), jnp.float32)
        kept = []
        for q in range(PIECES):
            span = slice(q * piece, (q + 1) * piece)
            routed = matmul_t(router_table, router_ref[span])
            normed_grad = (summed[q * tokens : (q + 1) * tokens] + routed) * gain_ref[:, span]
            inner += jnp.sum(
                acts[m, :, span].astype(jnp.float32) * normed_grad, axis=1, keepdims=True
            )
            kept.append(normed_grad)
        inner = scale * scale * scale * (inner / width)
        for q in range(PIECES):
            span = slice(q * piece, (q + 1) * piece)
            result = grads[m, :, span].astype(jnp.float32) + scale * kept[q]
            result -= acts[m, :, span].astype(jnp.float32) * inner
            grad_ref[m, :, span] = result.astype(jnp.bfloat16)

        @pl.when(section > 0)
        def _():
            pltpu.make_async_remote_copy(
                src_ref=grad_ref.at[m],
                dst_ref=grads.at[m],
                send_sem=pipe_sem.at[1],
                recv_sem=grad_sem.at[m],
                device_id={"pipe": section - 1},
                device_id_type=MESH,
            ).start()

    to_expert, to_finish, stage = offsets
    turn = sections * stage
    forward_at = section * stage
    backward_at = turn + (sections - 1 - section) * stage
    steps = {
        "FA": (forward_send, forward_at),
        "FB": (forward_expert, forward_at + to_expert),
        "FC": (forward_finish, forward_at + to_finish),
        "BA": (backward_send, backward_at),
        "BB": (backward_expert, backward_at + to_expert),
        "BC": (backward_finish, backward_at + to_finish),
    }

    for copy in weights:
        copy.wait()

    def slot_body(i, carry):
        for name in slots:
            step, begin = steps[name]
            m = i - begin

            @pl.when((m >= 0) & (m < micro_count))
            def _():
                step(m)

        return carry

    last = turn + (sections - 1) * stage + to_finish + micro_count
    lax.fori_loop(0, last, slot_body, 0)

    @pl.when(section < sections - 1)
    def _():
        wait_all(out_ref, pipe_sem.at[0])

    @pl.when(section > 0)
    def _():
        wait_all(grad_ref, pipe_sem.at[1])


def routing_tables(ids, chips, capacity):
    lines, columns = grid_of(chips)
    micro_count, tokens, top_count = ids.shape
    chip = lax.axis_index("expert") // 2
    flat = ids.reshape(micro_count, tokens * top_count)
    number = jnp.arange(tokens * top_count)
    same = (flat[:, :, None] == flat[:, None, :]) & (number[None, None, :] < number[None, :, None])
    rank = jnp.sum(same.astype(jnp.int32), axis=2).reshape(ids.shape)
    to_line = (ids // columns - chip // columns + lines) % lines
    to_column = (ids % columns - chip % columns + columns) % columns
    place = (to_line * columns + to_column) * block_rows(capacity) + rank
    place = jnp.moveaxis(place, 2, 1)[:, :, None, :]
    place = place + (jnp.arange(PIECES, dtype=jnp.int32) * capacity)[None, None, :, None]
    flat_place = place.reshape(micro_count, top_count * PIECES * tokens)
    return flat_place[:, None, :], flat_place[:, :, None], jnp.moveaxis(ids, 2, 1)[..., None]


OFFSETS = (1, 3, 4)
SLOTS = ("FC", "BC", "FA", "BA", "FB", "BB")


def on_device(
    inputs, cotangent, norm_gain, router_weight, gate_weight, up_weight, down_weight, route_ids
):
    sections = lax.axis_size("pipe")
    chips = lax.axis_size("expert") // 2
    micro_count, tokens, width = inputs.shape
    experts = router_weight.shape[2]
    top_count = route_ids.shape[3]
    capacity = min(tokens, (5 * tokens * top_count + 4 * experts - 1) // (4 * experts))
    hidden = gate_weight.shape[2]
    block = block_rows(capacity)
    piece = width // PIECES
    group = chips * capacity
    tables = routing_tables(route_ids[0], chips, capacity)
    anywhere = pl.BlockSpec(memory_space=pl.ANY)
    inside = pl.BlockSpec(memory_space=pltpu.VMEM)
    bf16, f32 = jnp.bfloat16, jnp.float32
    out = jax.ShapeDtypeStruct((micro_count, tokens, width), bf16)
    dma = pltpu.SemaphoreType.DMA
    geometry = (sections, micro_count, chips, capacity, OFFSETS, SLOTS)
    forward_out, backward_out = pl.pallas_call(
        functools.partial(relay_kernel, geometry),
        out_shape=(out, out),
        in_specs=[anywhere] * 2 + [inside] * 2 + [anywhere] * 3 + [inside] * 3,
        out_specs=(inside, inside),
        scratch_shapes=[
            pltpu.VMEM((width, hidden), bf16),
            pltpu.VMEM((width, hidden), bf16),
            pltpu.VMEM((hidden, width), bf16),
            pltpu.VMEM((micro_count, tokens, width), bf16),
            pltpu.VMEM((micro_count, tokens, width), bf16),
            pltpu.VMEM((PIECES * group, chips * block), bf16),
            pltpu.VMEM((chips * block, PIECES * group), bf16),
            pltpu.VMEM((4, chips, block, piece), bf16),
            pltpu.VMEM((micro_count, chips, block, piece), bf16),
            pltpu.VMEM((micro_count, chips, block, piece), bf16),
            pltpu.VMEM((4, chips, block, piece), bf16),
            pltpu.VMEM((micro_count, chips, block, piece), bf16),
            pltpu.VMEM((PIECES, group, piece), bf16),
            pltpu.VMEM((PIECES, group, piece), bf16),
            pltpu.VMEM((micro_count, PIECES, group, piece), bf16),
            pltpu.VMEM((PIECES, 2 * group, piece), bf16),
            pltpu.VMEM((micro_count, 2 * group, hidden), f32),
            pltpu.VMEM((micro_count, 2 * group, hidden), f32),
            pltpu.VMEM((micro_count, top_count, tokens, width), bf16),
            pltpu.VMEM((micro_count, 7, tokens, 1), f32),
            dma((3,)),
            dma((micro_count,)),
            dma((micro_count,)),
            dma((2,)),
            dma((4,)),
            dma((micro_count,)),
            dma,
            dma((micro_count,)),
            dma,
            dma((micro_count,)),
            dma((4,)),
            dma((micro_count,)),
        ],
        compiler_params=pltpu.CompilerParams(
            collective_id=0, has_side_effects=True, vmem_limit_bytes=66_000_000
        ),
    )(
        inputs,
        cotangent,
        norm_gain,
        router_weight[0],
        gate_weight[0],
        up_weight[0],
        down_weight[0],
        *tables,
    )
    return (forward_out[None], backward_out[None])


def solution(mesh):
    return jax.shard_map(
        on_device,
        mesh=mesh,
        in_specs=(
            P(None, "expert", None),
            P(None, "expert", None),
            P("pipe", None),
            P("pipe", None, None),
            P("pipe", None, "expert"),
            P("pipe", None, "expert"),
            P("pipe", "expert", None),
            P("pipe", None, "expert", None),
        ),
        out_specs=(P("pipe", None, "expert", None), P("pipe", None, "expert", None)),
        check_vma=False,
    )
```

```python
import functools
import math

import jax
import jax.numpy as jnp
from jax import lax
from jax.experimental import pallas as pl
from jax.experimental.pallas import tpu as pltpu
from jax.sharding import PartitionSpec as P

EPSILON = 1e-06
PIECES = 7
CHUNKS = 2
MESH = pl.DeviceIdType.MESH


def grid_of(chips):
    rows = math.isqrt(chips)
    while chips % rows:
        rows -= 1
    return rows, chips // rows


def block_rows(capacity):
    return -(-PIECES * capacity // 8) * 8


def matmul(left, right):
    return jnp.dot(left, right, preferred_element_type=jnp.float32)


def matmul_t(left, right):
    return lax.dot_general(
        left, right, (((1,), (1,)), ((), ())), preferred_element_type=jnp.float32
    )


def relay_kernel(
    geometry,
    inputs_ref,
    cotangent_ref,
    gain_ref,
    router_ref,
    wg_hbm,
    wu_hbm,
    wd_hbm,
    row_table_ref,
    col_table_ref,
    ids_ref,
    out_ref,
    grad_ref,
    wg,
    wu,
    wd,
    acts,
    grads,
    unpack,
    repack,
    dispatch_send,
    dispatch_recv,
    partner_rows,
    combine_send,
    combine_recv,
    half_send,
    half_own,
    half_recv,
    rows_in,
    squares,
    gate_saved,
    up_saved,
    hidden_grad,
    picked,
    kept,
    stats,
    weight_sem,
    act_sem,
    grad_sem,
    pipe_sem,
    dispatch_send_sem,
    dispatch_recv_sem,
    swap_send_sem,
    swap_recv_sem,
    half_send_sem,
    half_recv_sem,
    combine_send_sem,
    combine_recv_sem,
):
    sections, micro_count, chips, capacity = geometry
    lines, columns = grid_of(chips)
    block = block_rows(capacity)
    tokens, part_width = acts.shape[2], acts.shape[3]
    width = CHUNKS * part_width
    piece = part_width // PIECES
    group = chips * capacity
    hidden = wg.shape[1]
    experts = router_ref.shape[1]
    lanes = PIECES * tokens
    section = lax.axis_index("pipe")
    place = lax.axis_index("expert")
    core = lax.rem(place, 2)
    chip = place // 2
    line, column = chip // columns, lax.rem(chip, columns)
    partner = chip * 2 + (1 - core)
    others = pl.ds(1, chips - 1)

    def peer(step, sign):
        to_line = lax.rem(line + sign * (step // columns) + lines, lines)
        to_column = lax.rem(column + sign * lax.rem(step, columns) + columns, columns)
        return {"expert": (to_line * columns + to_column) * 2 + core}

    def span(c):
        return slice(c * part_width, (c + 1) * part_width)

    def pieces_of(value):
        return [value[:, q * piece : (q + 1) * piece] for q in range(PIECES)]

    barrier = pltpu.get_barrier_semaphore()

    def greet(step, carry):
        pl.semaphore_signal(barrier, inc=1, device_id=peer(step, 1), device_id_type=MESH)
        return carry

    weights = [
        pltpu.make_async_copy(source, target, weight_sem.at[i])
        for i, (source, target) in enumerate([(wg_hbm, wg), (wu_hbm, wu), (wd_hbm, wd)])
    ]

    def fetch(source, target, semaphore):
        for m in range(micro_count):
            for c in range(CHUNKS):
                pltpu.make_async_copy(
                    source.at[m, :, span(c)], target.at[m, c], semaphore.at[m * CHUNKS + c]
                ).start()

    @pl.when(section == 0)
    def _():
        fetch(inputs_ref, acts, act_sem)

    @pl.when(section == sections - 1)
    def _():
        fetch(cotangent_ref, grads, grad_sem)

    for copy in weights:
        copy.start()
    lax.fori_loop(1, chips, greet, 0)
    pl.semaphore_signal(barrier, inc=1, device_id={"expert": partner}, device_id_type=MESH)
    for sign in (1, sections - 1):
        pl.semaphore_signal(
            barrier,
            inc=1,
            device_id={"pipe": lax.rem(section + sign, sections)},
            device_id_type=MESH,
        )

    def place_of(number):
        within = lax.rem(number, block)
        q = within // capacity
        row = q * group + (number // block) * capacity + lax.rem(within, capacity)
        return jnp.where(within < PIECES * capacity, row, -1)

    shape = (PIECES * group, chips * block)
    wide = place_of(lax.broadcasted_iota(jnp.int32, (1, shape[1]), 1))
    unpack[...] = jnp.where(
        lax.broadcasted_iota(jnp.int32, shape, 0) == wide, 1.0, 0.0
    ).astype(jnp.bfloat16)
    tall = place_of(lax.broadcasted_iota(jnp.int32, (shape[1], 1), 0))
    repack[...] = jnp.where(
        lax.broadcasted_iota(jnp.int32, shape[::-1], 1) == tall, 1.0, 0.0
    ).astype(jnp.bfloat16)

    pl.semaphore_wait(barrier, chips - 1 + 1 + 2)

    def wait_all(buffer, semaphore):
        pltpu.make_async_copy(buffer, buffer, semaphore).wait()

    def post(values, m, c, send, recv, send_sem, recv_sem, sign):
        values = values.astype(jnp.bfloat16).reshape(chips, block, piece)
        recv[m, c, 0] = values[0]
        send[m, c, others] = values[1:]

        def start(step, carry):
            pltpu.make_async_remote_copy(
                src_ref=send.at[m, c, step],
                dst_ref=recv.at[m, c, step],
                send_sem=send_sem.at[m * CHUNKS + c],
                recv_sem=recv_sem.at[m * CHUNKS + c],
                device_id=peer(step, sign),
                device_id_type=MESH,
            ).start()
            return carry

        lax.fori_loop(1, chips, start, 0)

    def dispatch(values, m, c):
        post(
            values, m, c, dispatch_send, dispatch_recv, dispatch_send_sem, dispatch_recv_sem, 1
        )

    def table_rows(m):
        rows = lax.broadcasted_iota(jnp.int32, (chips * block, 2 * lanes), 0)
        return jnp.where(rows == row_table_ref[m], 1.0, 0.0).astype(jnp.bfloat16)

    def table_columns(m):
        places = lax.broadcasted_iota(jnp.int32, (2 * lanes, chips * block), 1)
        return jnp.where(places == col_table_ref[m], 1.0, 0.0).astype(jnp.bfloat16)

    def expert_hot(m, k):
        names = lax.broadcasted_iota(jnp.int32, (tokens, experts), 1)
        return jnp.where(names == ids_ref[m, k], 1.0, 0.0)

    def take_rows(m, c, way):
        number = m * CHUNKS + c
        wait_all(dispatch_recv.at[m, c, others], dispatch_recv_sem.at[number])
        swap = pltpu.make_async_remote_copy(
            src_ref=dispatch_recv.at[m, c],
            dst_ref=partner_rows.at[m, c],
            send_sem=swap_send_sem,
            recv_sem=swap_recv_sem.at[number],
            device_id={"expert": partner},
            device_id_type=MESH,
        )
        swap.start()
        wait_all(dispatch_send.at[m, c, others], dispatch_send_sem.at[number])
        for part, source in enumerate((dispatch_recv, partner_rows)):
            if part == 1:
                swap.wait()
            rows = matmul(unpack[...], source[m, c].reshape(chips * block, piece))
            mine = slice(part * group, (part + 1) * group)
            square = jnp.zeros((group, piece), jnp.float32)
            for q in range(PIECES):
                at = slice(c * part_width + q * piece, c * part_width + (q + 1) * piece)
                found = rows[q * group : (q + 1) * group]
                if way == 0:
                    square += found * found
                    found = found * gain_ref[:, at]
                rows_in[way, mine, at] = found.astype(jnp.bfloat16)
            if way == 0:
                square = jnp.sum(square, axis=1, keepdims=True)
                squares[mine] = square if c == 0 else squares[mine] + square

    def halves_and_combine(m, product):
        copies = []
        for c in range(CHUNKS):
            part = product(c).astype(jnp.bfloat16)
            for q, values in enumerate(pieces_of(part)):
                half_own[c, q] = values[:group]
                half_send[c, q] = values[group:]
            copy = pltpu.make_async_remote_copy(
                src_ref=half_send.at[c],
                dst_ref=half_recv.at[m, c],
                send_sem=half_send_sem.at[c],
                recv_sem=half_recv_sem.at[m * CHUNKS + c],
                device_id={"expert": partner},
                device_id_type=MESH,
            )
            copy.start()
            copies.append(copy)
        for c in range(CHUNKS):
            copies[c].wait()
            total = half_own[c].astype(jnp.float32) + half_recv[m, c].astype(jnp.float32)
            total = total.astype(jnp.bfloat16).reshape(PIECES * group, piece)
            post(
                matmul(repack[...], total),
                m,
                c,
                combine_send,
                combine_recv,
                combine_send_sem,
                combine_recv_sem,
                -1,
            )

    def forward_send(m, c):
        wait_all(acts.at[m, c], act_sem.at[m * CHUNKS + c])
        table = table_rows(m)
        stacked = jnp.concatenate(pieces_of(acts[m, c]), axis=0)
        dispatch(matmul(table[:, :lanes] + table[:, lanes:], stacked), m, c)
        if c < CHUNKS - 1:
            return
        square = jnp.zeros((tokens, 1), jnp.float32)
        for d in range(CHUNKS):
            wide_in = acts[m, d].astype(jnp.float32)
            square += jnp.sum(wide_in * wide_in, axis=1, keepdims=True)
        scale = lax.rsqrt(square / width + EPSILON)
        logits = jnp.zeros((tokens, experts), jnp.float32)
        for d in range(CHUNKS):
            wide_in = acts[m, d].astype(jnp.float32)
            normed = (wide_in * scale * gain_ref[:, span(d)]).astype(jnp.bfloat16)
            logits += matmul(normed, router_ref[span(d)])
        chances = []
        for k in range(2):
            score = jnp.sum(logits * expert_hot(m, k), axis=1, keepdims=True)
            chances.append(1.0 / (1.0 + jnp.exp(-score)))
        total = chances[0] + chances[1]
        stats[m, 0] = scale
        stats[m, 1] = chances[0]
        stats[m, 2] = chances[1]
        stats[m, 3] = chances[0] / total
        stats[m, 4] = chances[1] / total

    def forward_expert(m, c):
        take_rows(m, c, 0)
        gate_pre = matmul(rows_in[0, :, span(c)], wg[span(c)])
        up_pre = matmul(rows_in[0, :, span(c)], wu[span(c)])
        if c > 0:
            gate_pre += gate_saved[m]
            up_pre += up_saved[m]
        if c < CHUNKS - 1:
            gate_saved[m] = gate_pre
            up_saved[m] = up_pre
            return
        scale = lax.rsqrt(squares[...] / width + EPSILON)
        gate_pre = gate_pre * scale
        up_pre = up_pre * scale
        gate_saved[m] = gate_pre
        up_saved[m] = up_pre
        inner = (gate_pre / (1.0 + jnp.exp(-gate_pre)) * up_pre).astype(jnp.bfloat16)
        halves_and_combine(m, lambda d: matmul(inner, wd[:, span(d)]))

    def receive_combined(m, c):
        number = m * CHUNKS + c
        wait_all(combine_recv.at[m, c, others], combine_recv_sem.at[number])
        wait_all(combine_send.at[m, c, others], combine_send_sem.at[number])
        return combine_recv[m, c].reshape(chips * block, piece)

    def forward_finish(m, c):
        found = matmul(table_columns(m), receive_combined(m, c))
        for q in range(PIECES):
            at = slice(q * piece, (q + 1) * piece)
            total = acts[m, c, :, at].astype(jnp.float32)
            for k in range(2):
                begin = (k * PIECES + q) * tokens
                rows = found[begin : begin + tokens]
                picked[m, c, k, :, at] = rows.astype(jnp.bfloat16)
                total += stats[m, 3 + k] * rows
            begin = c * part_width + q * piece
            out_ref[m, :, begin : begin + piece] = total.astype(jnp.bfloat16)

        @pl.when(section < sections - 1)
        def _():
            pltpu.make_async_remote_copy(
                src_ref=out_ref.at[m, :, span(c)],
                dst_ref=acts.at[m, c],
                send_sem=pipe_sem.at[0],
                recv_sem=act_sem.at[m * CHUNKS + c],
                device_id={"pipe": section + 1},
                device_id_type=MESH,
            ).start()

    def backward_send(m, c):
        wait_all(grads.at[m, c], grad_sem.at[m * CHUNKS + c])
        upstream = grads[m, c].astype(jnp.float32)
        stacked = []
        for k in range(2):
            stacked += pieces_of((stats[m, 3 + k] * upstream).astype(jnp.bfloat16))
        dispatch(matmul(table_rows(m), jnp.concatenate(stacked, axis=0)), m, c)
        slopes = []
        for k in range(2):
            values = picked[m, c, k].astype(jnp.float32)
            slope = jnp.sum(upstream * values, axis=1, keepdims=True)
            slopes.append(slope if c == 0 else slope + stats[m, 5 + k])
        if c == CHUNKS - 1:
            weighted = stats[m, 3] * slopes[0] + stats[m, 4] * slopes[1]
            total = stats[m, 1] + stats[m, 2]
            for k in range(2):
                chance = stats[m, 1 + k]
                slopes[k] = (slopes[k] - weighted) / total * chance * (1.0 - chance)
        for k in range(2):
            stats[m, 5 + k] = slopes[k]

    def backward_expert(m, c):
        take_rows(m, c, 1)
        inner_grad = matmul_t(rows_in[1, :, span(c)], wd[:, span(c)])
        if c > 0:
            inner_grad += hidden_grad[...]
        if c < CHUNKS - 1:
            hidden_grad[...] = inner_grad
            return
        gate_pre = gate_saved[m]
        sigmoid = 1.0 / (1.0 + jnp.exp(-gate_pre))
        pre_grad = (
            inner_grad * up_saved[m] * sigmoid * (1.0 + gate_pre * (1.0 - sigmoid))
        ).astype(jnp.bfloat16)
        up_grad = (inner_grad * gate_pre * sigmoid).astype(jnp.bfloat16)
        halves_and_combine(
            m, lambda d: matmul_t(pre_grad, wg[span(d)]) + matmul_t(up_grad, wu[span(d)])
        )

    def backward_finish(m, c):
        table = table_columns(m)
        summed = matmul(table[:lanes] + table[lanes:], receive_combined(m, c))
        router_table = (
            stats[m, 5] * expert_hot(m, 0) + stats[m, 6] * expert_hot(m, 1)
        ).astype(jnp.bfloat16)
        routed = matmul_t(router_table, router_ref[span(c)])
        inner = jnp.zeros((tokens, piece), jnp.float32)
        for q in range(PIECES):
            at = slice(q * piece, (q + 1) * piece)
            begin = c * part_width + q * piece
            normed_grad = summed[q * tokens : (q + 1) * tokens] + routed[:, at]
            normed_grad = normed_grad * gain_ref[:, begin : begin + piece]
            inner += acts[m, c, :, at].astype(jnp.float32) * normed_grad
            kept[c, :, at] = normed_grad
        inner = jnp.sum(inner, axis=1, keepdims=True)
        if c < CHUNKS - 1:
            stats[m, 7] = inner
            return
        scale = stats[m, 0]
        inner = scale * scale * scale * ((inner + stats[m, 7]) / width)
        for d in range(CHUNKS):
            result = grads[m, d].astype(jnp.float32) + scale * kept[d]
            result -= acts[m, d].astype(jnp.float32) * inner
            grad_ref[m, :, span(d)] = result.astype(jnp.bfloat16)

            @pl.when(section > 0)
            def _():
                pltpu.make_async_remote_copy(
                    src_ref=grad_ref.at[m, :, span(d)],
                    dst_ref=grads.at[m, d],
                    send_sem=pipe_sem.at[1],
                    recv_sem=grad_sem.at[m * CHUNKS + d],
                    device_id={"pipe": section - 1},
                    device_id_type=MESH,
                ).start()

    for copy in weights:
        copy.wait()
    steps = (
        forward_send,
        forward_expert,
        forward_finish,
        backward_send,
        backward_expert,
        backward_finish,
    )
    words = order_words(sections, micro_count)

    def run(i, counts):
        word = jnp.int32(0)
        for s, row in enumerate(words):
            for w, number in enumerate(row):
                word = jnp.where((section == s) & (i // DIGITS == w), number, word)
        word = lax.fori_loop(0, lax.rem(i, DIGITS), lambda j, rest: rest // 8, word)
        kind = lax.rem(word, 8)
        for number, step in enumerate(steps):
            m, c = counts[number] // CHUNKS, lax.rem(counts[number], CHUNKS)
            for d in range(CHUNKS):

                @pl.when((kind == number) & (c == d))
                def _():
                    step(m, d)

        return tuple(
            count + jnp.where(kind == number, 1, 0) for number, count in enumerate(counts)
        )

    total_steps = 6 * micro_count * CHUNKS
    lax.fori_loop(0, total_steps, run, (jnp.int32(0),) * 6)

    @pl.when(section < sections - 1)
    def _():
        wait_all(out_ref, pipe_sem.at[0])

    @pl.when(section > 0)
    def _():
        wait_all(grad_ref, pipe_sem.at[1])


KINDS = "abcABC"
DIGITS = 10
ORDERS = (
    "aaaabbbbcaacaaccbbbbccccAABBACACBBACACBBACACBBCC",
    "aaababbbccacacababbbccccAABBACACBBACACBBACACBBCC",
    "aaababbbccacacababbbccccAABBAACCBBAACCBBAACCBBCC",
    "aaababbbccAAcaacABABbbBBCaCaccAACCbbBBccAACCBBCC",
)


def order_words(sections, micro_count):
    orders = ORDERS
    if (sections, micro_count) != (4, 4):
        orders = ("aabbcc" * micro_count + "AABBCC" * micro_count,) * sections
    words = []
    for order in orders:
        row = []
        for begin in range(0, len(order), DIGITS):
            digits = [KINDS.index(kind) for kind in order[begin : begin + DIGITS]]
            row.append(sum(digit * 8**j for j, digit in enumerate(digits)))
        words.append(row)
    return words


def routing_tables(ids, chips, capacity):
    lines, columns = grid_of(chips)
    micro_count, tokens, top_count = ids.shape
    chip = lax.axis_index("expert") // 2
    flat = ids.reshape(micro_count, tokens * top_count)
    number = jnp.arange(tokens * top_count)
    same = (flat[:, :, None] == flat[:, None, :]) & (number[None, None, :] < number[None, :, None])
    rank = jnp.sum(same.astype(jnp.int32), axis=2).reshape(ids.shape)
    to_line = (ids // columns - chip // columns + lines) % lines
    to_column = (ids % columns - chip % columns + columns) % columns
    place = (to_line * columns + to_column) * block_rows(capacity) + rank
    place = jnp.moveaxis(place, 2, 1)[:, :, None, :]
    place = place + (jnp.arange(PIECES, dtype=jnp.int32) * capacity)[None, None, :, None]
    flat_place = place.reshape(micro_count, top_count * PIECES * tokens)
    return flat_place[:, None, :], flat_place[:, :, None], jnp.moveaxis(ids, 2, 1)[..., None]


def on_device(
    inputs, cotangent, norm_gain, router_weight, gate_weight, up_weight, down_weight, route_ids
):
    sections = lax.axis_size("pipe")
    chips = lax.axis_size("expert") // 2
    micro_count, tokens, width = inputs.shape
    experts = router_weight.shape[2]
    top_count = route_ids.shape[3]
    capacity = min(tokens, (5 * tokens * top_count + 4 * experts - 1) // (4 * experts))
    hidden = gate_weight.shape[2]
    block = block_rows(capacity)
    part_width = width // CHUNKS
    piece = part_width // PIECES
    group = chips * capacity
    tables = routing_tables(route_ids[0], chips, capacity)
    anywhere = pl.BlockSpec(memory_space=pl.ANY)
    inside = pl.BlockSpec(memory_space=pltpu.VMEM)
    bf16, f32 = jnp.bfloat16, jnp.float32
    out = jax.ShapeDtypeStruct((micro_count, tokens, width), bf16)
    dma = pltpu.SemaphoreType.DMA
    geometry = (sections, micro_count, chips, capacity)
    blocks = (micro_count, CHUNKS, chips, block, piece)
    halves = (CHUNKS, PIECES, group, piece)
    parts = micro_count * CHUNKS
    forward_out, backward_out = pl.pallas_call(
        functools.partial(relay_kernel, geometry),
        out_shape=(out, out),
        in_specs=[anywhere] * 2 + [inside] * 2 + [anywhere] * 3 + [inside] * 3,
        out_specs=(inside, inside),
        scratch_shapes=[
            pltpu.VMEM((width, hidden), bf16),
            pltpu.VMEM((width, hidden), bf16),
            pltpu.VMEM((hidden, width), bf16),
            pltpu.VMEM((micro_count, CHUNKS, tokens, part_width), bf16),
            pltpu.VMEM((micro_count, CHUNKS, tokens, part_width), bf16),
            pltpu.VMEM((PIECES * group, chips * block), bf16),
            pltpu.VMEM((chips * block, PIECES * group), bf16),
            pltpu.VMEM(blocks, bf16),
            pltpu.VMEM(blocks, bf16),
            pltpu.VMEM(blocks, bf16),
            pltpu.VMEM(blocks, bf16),
            pltpu.VMEM(blocks, bf16),
            pltpu.VMEM(halves, bf16),
            pltpu.VMEM(halves, bf16),
            pltpu.VMEM((micro_count, *halves), bf16),
            pltpu.VMEM((2, 2 * group, width), bf16),
            pltpu.VMEM((2 * group, 1), f32),
            pltpu.VMEM((micro_count, 2 * group, hidden), f32),
            pltpu.VMEM((micro_count, 2 * group, hidden), f32),
            pltpu.VMEM((2 * group, hidden), f32),
            pltpu.VMEM((micro_count, CHUNKS, top_count, tokens, part_width), bf16),
            pltpu.VMEM((CHUNKS, tokens, part_width), f32),
            pltpu.VMEM((micro_count, 8, tokens, 1), f32),
            dma((3,)),
            dma((parts,)),
            dma((parts,)),
            dma((2,)),
            dma((parts,)),
            dma((parts,)),
            dma,
            dma((parts,)),
            dma((CHUNKS,)),
            dma((parts,)),
            dma((parts,)),
            dma((parts,)),
        ],
        compiler_params=pltpu.CompilerParams(
            collective_id=0, has_side_effects=True, vmem_limit_bytes=66_000_000
        ),
    )(
        inputs,
        cotangent,
        norm_gain,
        router_weight[0],
        gate_weight[0],
        up_weight[0],
        down_weight[0],
        *tables,
    )
    return (forward_out[None], backward_out[None])


def solution(mesh):
    return jax.shard_map(
        on_device,
        mesh=mesh,
        in_specs=(
            P(None, "expert", None),
            P(None, "expert", None),
            P("pipe", None),
            P("pipe", None, None),
            P("pipe", None, "expert"),
            P("pipe", None, "expert"),
            P("pipe", "expert", None),
            P("pipe", None, "expert", None),
        ),
        out_specs=(P("pipe", None, "expert", None), P("pipe", None, "expert", None)),
        check_vma=False,
    )
```

```python
import functools
import math

import jax
import jax.numpy as jnp
from jax import lax
from jax.experimental import pallas as pl
from jax.experimental.pallas import tpu as pltpu
from jax.sharding import PartitionSpec as P

EPSILON = 1e-06
CHUNK_PIECES = (8, 6)
CHUNKS = len(CHUNK_PIECES)
MESH = pl.DeviceIdType.MESH


def grid_of(chips):
    rows = math.isqrt(chips)
    while chips % rows:
        rows -= 1
    return rows, chips // rows


def block_rows(c, capacity):
    return -(-CHUNK_PIECES[c] * capacity // 8) * 8


def matmul(left, right):
    return jnp.dot(left, right, preferred_element_type=jnp.float32)


def matmul_t(left, right):
    return lax.dot_general(
        left, right, (((1,), (1,)), ((), ())), preferred_element_type=jnp.float32
    )


def relay_kernel(
    geometry,
    inputs_ref,
    cotangent_ref,
    gain_ref,
    router_ref,
    wg_hbm,
    wu_hbm,
    wd_hbm,
    ids_ref,
    out_ref,
    grad_ref,
    wg,
    wu,
    wd,
    acts,
    grads,
    unpack,
    repack,
    slot_pick,
    row_place,
    column_place,
    slot_place,
    dispatch_send,
    dispatch_recv,
    partner_rows,
    combine_send,
    combine_recv,
    half_send,
    half_own,
    half_recv,
    gate_send,
    gate_recv,
    rows_in,
    squares,
    gate_saved,
    up_saved,
    hidden_grad,
    picked,
    kept,
    stats,
    weight_sem,
    act_sem,
    grad_sem,
    pipe_sem,
    dispatch_send_sem,
    dispatch_recv_sem,
    swap_send_sem,
    swap_recv_sem,
    half_send_sem,
    half_recv_sem,
    combine_send_sem,
    combine_recv_sem,
    gate_send_sem,
    gate_recv_sem,
):
    sections, micro_count, chips, capacity = geometry
    lines, columns = grid_of(chips)
    tokens, width = acts.shape[1], acts.shape[2]
    piece = width // sum(CHUNK_PIECES)
    group = chips * capacity
    slots = gate_send.shape[2]
    hidden = wg.shape[1]
    experts = router_ref.shape[0]
    bf16, f32 = jnp.bfloat16, jnp.float32
    section = lax.axis_index("pipe")
    place = lax.axis_index("expert")
    core = lax.rem(place, 2)
    chip = place // 2
    line, column = chip // columns, lax.rem(chip, columns)
    partner = chip * 2 + (1 - core)
    others = pl.ds(1, chips - 1)

    def peer(step, sign, to_core=core):
        to_line = lax.rem(line + sign * (step // columns) + lines, lines)
        to_column = lax.rem(column + sign * lax.rem(step, columns) + columns, columns)
        return {"expert": (to_line * columns + to_column) * 2 + to_core}

    def begin_of(c, q=0):
        return (sum(CHUNK_PIECES[:c]) + q) * piece

    def span(c):
        return slice(begin_of(c), begin_of(c + 1))

    def pieces_of(value):
        return [value[:, q : q + piece] for q in range(0, value.shape[1], piece)]

    def block_of(c):
        return block_rows(c, capacity)

    barrier = pltpu.get_barrier_semaphore()

    def greet(step, carry):
        for to_core in (core, 1 - core):
            pl.semaphore_signal(
                barrier, inc=1, device_id=peer(step, 1, to_core), device_id_type=MESH
            )
        return carry

    weights = [
        pltpu.make_async_copy(source, target, weight_sem.at[i])
        for i, (source, target) in enumerate([(wg_hbm, wg), (wu_hbm, wu), (wd_hbm, wd)])
    ]

    def fetch(source, target, semaphore):
        for m in range(micro_count):
            for c in range(CHUNKS):
                pltpu.make_async_copy(
                    source.at[m, :, span(c)],
                    target.at[m, :, span(c)],
                    semaphore.at[m * CHUNKS + c],
                ).start()

    @pl.when(section == 0)
    def _():
        fetch(inputs_ref, acts, act_sem)

    @pl.when(section == sections - 1)
    def _():
        fetch(cotangent_ref, grads, grad_sem)

    for copy in weights:
        copy.start()
    lax.fori_loop(1, chips, greet, 0)
    pl.semaphore_signal(barrier, inc=1, device_id={"expert": partner}, device_id_type=MESH)
    for sign in (1, sections - 1):
        pl.semaphore_signal(
            barrier,
            inc=1,
            device_id={"pipe": lax.rem(section + sign, sections)},
            device_id_type=MESH,
        )

    def iota(shape, axis):
        return lax.broadcasted_iota(jnp.int32, shape, axis)

    def hot(condition):
        return jnp.where(condition, 1.0, 0.0).astype(bf16)

    for c in range(CHUNKS):

        def place_of(number):
            within = lax.rem(number, block_of(c))
            q = within // capacity
            row = q * group + (number // block_of(c)) * capacity + lax.rem(within, capacity)
            return jnp.where(within < CHUNK_PIECES[c] * capacity, row, -1)

        shape = (CHUNK_PIECES[c] * group, chips * block_of(c))
        unpack[c][...] = hot(iota(shape, 0) == place_of(iota((1, shape[1]), 1)))
        repack[c][...] = hot(iota(shape[::-1], 1) == place_of(iota((shape[1], 1), 0)))
    shape = (group, chips * slots)
    wanted = iota((group, 1), 0)
    wanted = (wanted // capacity) * slots + lax.rem(wanted, capacity)
    slot_pick[...] = hot(iota(shape, 1) == wanted)

    earlier = hot(iota((tokens, tokens), 0) < iota((tokens, tokens), 1))
    for m in range(micro_count):
        ids = ids_ref[m]
        found = [hot(iota((experts, tokens), 0) == ids[k : k + 1]) for k in range(2)]
        counts = matmul(found[0] + found[1], earlier)
        ranks = [
            jnp.sum(counts * found[k].astype(f32), axis=0, keepdims=True) for k in range(2)
        ]
        ranks = jnp.concatenate(ranks, axis=0)
        to_line = lax.rem(ids // columns - line + lines, lines)
        to_column = lax.rem(lax.rem(ids, columns) - column + columns, columns)
        steps_to = (to_line * columns + to_column).astype(f32).astype(bf16)
        ranks_to = ranks.astype(bf16)
        for c in range(CHUNKS):
            lanes = CHUNK_PIECES[c] * tokens
            across = hot(iota((tokens, lanes), 0) == lax.rem(iota((1, lanes), 1), tokens))
            down = hot(lax.rem(iota((lanes, 1), 0), tokens) == iota((lanes, tokens), 1))
            where = matmul(steps_to, across).astype(jnp.int32) * block_of(c)
            where += matmul(ranks_to, across).astype(jnp.int32)
            row_place[c][m] = where + (iota((1, lanes), 1) // tokens) * capacity
            where = matmul_t(down, steps_to).astype(jnp.int32) * block_of(c)
            where += matmul_t(down, ranks_to).astype(jnp.int32)
            column_place[c][m] = where + (iota((lanes, 1), 0) // tokens) * capacity
        slot_place[m] = (steps_to.astype(f32) * slots + ranks).astype(jnp.int32)

    pl.semaphore_wait(barrier, 2 * (chips - 1) + 1 + 2)

    def wait_all(buffer, semaphore):
        pltpu.make_async_copy(buffer, buffer, semaphore).wait()

    def post(values, m, c, send, recv, send_sem, recv_sem, sign):
        values = values.astype(bf16).reshape(chips, block_of(c), piece)
        recv[m, 0] = values[0]
        send[m, others] = values[1:]

        def start(step, carry):
            pltpu.make_async_remote_copy(
                src_ref=send.at[m, step],
                dst_ref=recv.at[m, step],
                send_sem=send_sem.at[m * CHUNKS + c],
                recv_sem=recv_sem.at[m * CHUNKS + c],
                device_id=peer(step, sign),
                device_id_type=MESH,
            ).start()
            return carry

        lax.fori_loop(1, chips, start, 0)

    def dispatch(stacked, m, c, way):
        target = row_place[c][m]
        rows = iota((chips * block_of(c), target.shape[1]), 0)
        table = hot(rows == target[0:1]) + hot(rows == target[1:2])
        post(
            matmul(table, stacked),
            m,
            c,
            dispatch_send[way][c],
            dispatch_recv[way][c],
            dispatch_send_sem.at[way],
            dispatch_recv_sem.at[way],
            1,
        )

    def expert_hot(m):
        same = hot(iota((tokens, tokens), 0) == iota((tokens, tokens), 1))
        names = matmul_t(same, ids_ref[m].astype(f32).astype(bf16)).astype(jnp.int32)
        return [
            jnp.where(iota((tokens, experts), 1) == names[:, k : k + 1], 1.0, 0.0)
            for k in range(2)
        ]

    def take_rows(m, c, way):
        number = m * CHUNKS + c
        send, recv = dispatch_send[way][c], dispatch_recv[way][c]
        wait_all(recv.at[m, others], dispatch_recv_sem.at[way, number])
        swap = pltpu.make_async_remote_copy(
            src_ref=recv.at[m],
            dst_ref=partner_rows[way][c].at[m],
            send_sem=swap_send_sem,
            recv_sem=swap_recv_sem.at[way, number],
            device_id={"expert": partner},
            device_id_type=MESH,
        )
        swap.start()
        wait_all(send.at[m, others], dispatch_send_sem.at[way, number])
        for part, source in enumerate((recv, partner_rows[way][c])):
            if part == 1:
                swap.wait()
            rows = matmul(unpack[c][...], source[m].reshape(chips * block_of(c), piece))
            mine = slice(part * group, (part + 1) * group)
            square = jnp.zeros((group, piece), f32)
            for q in range(CHUNK_PIECES[c]):
                at = slice(begin_of(c, q), begin_of(c, q + 1))
                found = rows[q * group : (q + 1) * group]
                if way == 0:
                    square += found * found
                    found = found * gain_ref[:, at]
                rows_in[way, mine, at] = found.astype(bf16)
            if way == 0:
                square = jnp.sum(square, axis=1, keepdims=True)
                squares[mine] = square if c == 0 else squares[mine] + square

    def halves_and_combine(m, way, product):
        copies = []
        for c in range(CHUNKS):
            part = product(c).astype(bf16)
            for q, values in enumerate(pieces_of(part)):
                half_own[c][q] = values[:group]
                half_send[c][q] = values[group:]
            copy = pltpu.make_async_remote_copy(
                src_ref=half_send[c],
                dst_ref=half_recv[way][c].at[m],
                send_sem=half_send_sem.at[c],
                recv_sem=half_recv_sem.at[way, m * CHUNKS + c],
                device_id={"expert": partner},
                device_id_type=MESH,
            )
            copy.start()
            copies.append(copy)
        for c in range(CHUNKS):
            copies[c].wait()
            total = half_own[c][...].astype(f32) + half_recv[way][c][m].astype(f32)
            total = total.astype(bf16).reshape(CHUNK_PIECES[c] * group, piece)
            post(
                matmul(repack[c][...], total),
                m,
                c,
                combine_send[way][c],
                combine_recv[way][c],
                combine_send_sem.at[way],
                combine_recv_sem.at[way],
                -1,
            )

    def send_gates(m, gates):
        target = slot_place[m]
        rows = iota((chips * slots, tokens), 0)
        tables = [hot(rows == target[k : k + 1]) for k in range(2)]
        spread = jnp.zeros((chips * slots, 128), f32)
        for k in range(2):
            value = jnp.broadcast_to(gates[k], (tokens, 128))
            high = value.astype(bf16)
            low = (value - high.astype(f32)).astype(bf16)
            spread += matmul(tables[k], high) + matmul(tables[k], low)
        spread = spread.reshape(chips, slots, 128)
        gate_send[m] = spread
        gate_recv[m, 0, 0] = spread[0]

        def copy_to(step, part):
            pltpu.make_async_remote_copy(
                src_ref=gate_send.at[m, step],
                dst_ref=gate_recv.at[m, part, step],
                send_sem=gate_send_sem.at[m, part],
                recv_sem=gate_recv_sem.at[m, part],
                device_id=peer(step, 1, core if part == 0 else 1 - core),
                device_id_type=MESH,
            ).start()

        def start(step, carry):
            copy_to(step, 0)
            copy_to(step, 1)
            return carry

        copy_to(0, 1)
        lax.fori_loop(1, chips, start, 0)

    def take_gates(m):
        gates = []
        for part, arrived in enumerate((others, pl.ds(0, chips))):
            wait_all(gate_recv.at[m, part, arrived], gate_recv_sem.at[m, part])
            wait_all(gate_send.at[m, arrived], gate_send_sem.at[m, part])
            value = gate_recv[m, part].reshape(chips * slots, 128)
            high = value.astype(bf16)
            low = (value - high.astype(f32)).astype(bf16)
            gates.append(matmul(slot_pick[...], high) + matmul(slot_pick[...], low))
        return jnp.concatenate(gates, axis=0)[:, :1]

    def forward_send(m, c):
        wait_all(acts.at[m, :, span(c)], act_sem.at[m * CHUNKS + c])
        dispatch(jnp.concatenate(pieces_of(acts[m, :, span(c)]), axis=0), m, c, 0)
        if c < CHUNKS - 1:
            return
        wide_in = acts[m].astype(f32)
        scale = lax.rsqrt(jnp.mean(wide_in * wide_in, axis=1, keepdims=True) + EPSILON)
        normed = (wide_in * scale * gain_ref[...]).astype(bf16)
        logits = matmul_t(normed, router_ref[...])
        chances = [
            1.0 / (1.0 + jnp.exp(-jnp.sum(logits * named, axis=1, keepdims=True)))
            for named in expert_hot(m)
        ]
        total = chances[0] + chances[1]
        gates = [chance / total for chance in chances]
        send_gates(m, gates)
        stats[m, 0] = scale
        for k in range(2):
            stats[m, 1 + k] = chances[k]
            stats[m, 3 + k] = gates[k]

    def forward_expert(m, c):
        if c == 0:

            @pl.when(m == 0)
            def _():
                for copy in weights:
                    copy.wait()

        take_rows(m, c, 0)
        gate_pre = matmul(rows_in[0, :, span(c)], wg[span(c)])
        up_pre = matmul(rows_in[0, :, span(c)], wu[span(c)])
        if c > 0:
            gate_pre += gate_saved[m]
            up_pre += up_saved[m]
        if c < CHUNKS - 1:
            gate_saved[m] = gate_pre
            up_saved[m] = up_pre
            return
        scale = lax.rsqrt(squares[...] / width + EPSILON)
        gate_pre = gate_pre * scale
        up_pre = up_pre * scale
        gate_saved[m] = gate_pre
        up_saved[m] = up_pre
        inner = (gate_pre / (1.0 + jnp.exp(-gate_pre)) * up_pre).astype(bf16)
        halves_and_combine(m, 0, lambda d: matmul(inner, wd[:, span(d)]))

    def receive_combined(m, c, way):
        number = m * CHUNKS + c
        recv = combine_recv[way][c]
        wait_all(recv.at[m, others], combine_recv_sem.at[way, number])
        wait_all(combine_send[way][c].at[m, others], combine_send_sem.at[way, number])
        return recv[m].reshape(chips * block_of(c), piece)

    def column_tables(m, c):
        target = column_place[c][m]
        places = iota((target.shape[0], chips * block_of(c)), 1)
        return [hot(places == target[:, k : k + 1]) for k in range(2)]

    def forward_finish(m, c):
        received = receive_combined(m, c, 0)
        found = [matmul(table, received) for table in column_tables(m, c)]
        for q in range(CHUNK_PIECES[c]):
            at = slice(begin_of(c, q), begin_of(c, q + 1))
            total = acts[m, :, at].astype(f32)
            for k in range(2):
                rows = found[k][q * tokens : (q + 1) * tokens]
                picked[m, k, :, at] = rows.astype(bf16)
                total += stats[m, 3 + k] * rows
            out_ref[m, :, at] = total.astype(bf16)

        @pl.when(section < sections - 1)
        def _():
            pltpu.make_async_remote_copy(
                src_ref=out_ref.at[m, :, span(c)],
                dst_ref=acts.at[m, :, span(c)],
                send_sem=pipe_sem.at[0],
                recv_sem=act_sem.at[m * CHUNKS + c],
                device_id={"pipe": section + 1},
                device_id_type=MESH,
            ).start()

    def backward_send(m, c):
        wait_all(grads.at[m, :, span(c)], grad_sem.at[m * CHUNKS + c])
        dispatch(jnp.concatenate(pieces_of(grads[m, :, span(c)]), axis=0), m, c, 1)

    def backward_expert(m, c):
        take_rows(m, c, 1)
        inner_grad = matmul_t(rows_in[1, :, span(c)], wd[:, span(c)])
        if c > 0:
            inner_grad += hidden_grad[...]
        if c < CHUNKS - 1:
            hidden_grad[...] = inner_grad
            return
        inner_grad = inner_grad * take_gates(m)
        gate_pre = gate_saved[m]
        sigmoid = 1.0 / (1.0 + jnp.exp(-gate_pre))
        pre_grad = (
            inner_grad * up_saved[m] * sigmoid * (1.0 + gate_pre * (1.0 - sigmoid))
        ).astype(bf16)
        up_grad = (inner_grad * gate_pre * sigmoid).astype(bf16)
        halves_and_combine(
            m, 1, lambda d: matmul_t(pre_grad, wg[span(d)]) + matmul_t(up_grad, wu[span(d)])
        )

    def score_slopes(m):
        upstream = grads[m].astype(f32)
        slopes = [
            jnp.sum(upstream * picked[m, k].astype(f32), axis=1, keepdims=True)
            for k in range(2)
        ]
        weighted = stats[m, 3] * slopes[0] + stats[m, 4] * slopes[1]
        total = stats[m, 1] + stats[m, 2]
        for k in range(2):
            chance = stats[m, 1 + k]
            stats[m, 5 + k] = (slopes[k] - weighted) / total * chance * (1.0 - chance)

    def backward_finish(m, c):
        if c == 0:
            score_slopes(m)
        named = expert_hot(m)
        router_table = (stats[m, 5] * named[0] + stats[m, 6] * named[1]).astype(bf16)
        routed = matmul(router_table, router_ref[:, span(c)])
        received = receive_combined(m, c, 1)
        tables = column_tables(m, c)
        summed = matmul(tables[0] + tables[1], received)
        inner = jnp.zeros((tokens, piece), f32)
        for q in range(CHUNK_PIECES[c]):
            at = slice(begin_of(c, q), begin_of(c, q + 1))
            near = slice(q * piece, (q + 1) * piece)
            normed_grad = summed[q * tokens : (q + 1) * tokens] + routed[:, near]
            normed_grad = normed_grad * gain_ref[:, at]
            inner += acts[m, :, at].astype(f32) * normed_grad
            kept[:, at] = normed_grad
        inner = jnp.sum(inner, axis=1, keepdims=True)
        if c > 0:
            inner += stats[m, 7]
        if c < CHUNKS - 1:
            stats[m, 7] = inner
            return
        scale = stats[m, 0]
        inner = scale * scale * scale * (inner / width)
        for d in range(CHUNKS):
            result = grads[m, :, span(d)].astype(f32) + scale * kept[:, span(d)]
            result -= acts[m, :, span(d)].astype(f32) * inner
            grad_ref[m, :, span(d)] = result.astype(bf16)

            @pl.when(section > 0)
            def _():
                pltpu.make_async_remote_copy(
                    src_ref=grad_ref.at[m, :, span(d)],
                    dst_ref=grads.at[m, :, span(d)],
                    send_sem=pipe_sem.at[1],
                    recv_sem=grad_sem.at[m * CHUNKS + d],
                    device_id={"pipe": section - 1},
                    device_id_type=MESH,
                ).start()

    steps = (
        forward_send,
        forward_expert,
        forward_finish,
        backward_send,
        backward_expert,
        backward_finish,
    )
    words = order_words(sections, micro_count)

    def run(i, counts):
        word = jnp.int32(0)
        for s, row in enumerate(words):
            for w, number in enumerate(row):
                word = jnp.where((section == s) & (i // DIGITS == w), number, word)
        word = lax.fori_loop(0, lax.rem(i, DIGITS), lambda j, rest: rest // 8, word)
        kind = lax.rem(word, 8)
        for number, step in enumerate(steps):
            m, c = counts[number] // CHUNKS, lax.rem(counts[number], CHUNKS)
            for d in range(CHUNKS):

                @pl.when((kind == number) & (c == d))
                def _():
                    step(m, d)

        return tuple(
            count + jnp.where(kind == number, 1, 0) for number, count in enumerate(counts)
        )

    total_steps = 6 * micro_count * CHUNKS
    lax.fori_loop(0, total_steps, run, (jnp.int32(0),) * 6)

    @pl.when(section < sections - 1)
    def _():
        wait_all(out_ref, pipe_sem.at[0])

    @pl.when(section > 0)
    def _():
        wait_all(grad_ref, pipe_sem.at[1])


KINDS = "abcABC"
DIGITS = 10
ORDERS = (
    "aaaabbbbcaacaaccbbbbccccAAABABBBCCCCAAAABBBBCCCC",
    "aaababbbccccaaaabbbbccccAAABABBBCCCCAAAABBBBCCCC",
    "aaababbbccccaaaabbbbccccAAABABBBCCCCAAABABBBCCCC",
    "AAAAAAAAaaaabbBBbbBBaaccCCccCaaCbbBBbcbBBcCcCcCC",
)


def order_words(sections, micro_count):
    orders = ORDERS
    if (sections, micro_count) != (4, 4):
        orders = ("aabbcc" * micro_count + "AABBCC" * micro_count,) * (sections - 1)
        orders += ("AA" * micro_count + "aabbcc" * micro_count + "BBCC" * micro_count,)
    words = []
    for order in orders:
        row = []
        for begin in range(0, len(order), DIGITS):
            digits = [KINDS.index(kind) for kind in order[begin : begin + DIGITS]]
            row.append(sum(digit * 8**j for j, digit in enumerate(digits)))
        words.append(row)
    return words


def on_device(
    inputs, cotangent, norm_gain, router_weight, gate_weight, up_weight, down_weight, route_ids
):
    sections = lax.axis_size("pipe")
    chips = lax.axis_size("expert") // 2
    micro_count, tokens, width = inputs.shape
    experts = router_weight.shape[2]
    top_count = route_ids.shape[3]
    capacity = min(tokens, (5 * tokens * top_count + 4 * experts - 1) // (4 * experts))
    hidden = gate_weight.shape[2]
    piece = width // sum(CHUNK_PIECES)
    group = chips * capacity
    slots = -(-capacity // 8) * 8
    anywhere = pl.BlockSpec(memory_space=pl.ANY)
    inside = pl.BlockSpec(memory_space=pltpu.VMEM)
    bf16, f32 = jnp.bfloat16, jnp.float32
    out = jax.ShapeDtypeStruct((micro_count, tokens, width), bf16)
    dma = pltpu.SemaphoreType.DMA
    geometry = (sections, micro_count, chips, capacity)

    def per_chunk(shape_of, ways=0):
        chunks = tuple(pltpu.VMEM(shape_of(c), bf16) for c in range(CHUNKS))
        return (chunks, chunks) if ways else chunks

    def rows_of(c):
        return CHUNK_PIECES[c] * group

    def blocks_of(c):
        return chips * block_rows(c, capacity)

    def lanes_of(c):
        return CHUNK_PIECES[c] * tokens

    def exchange(c):
        return (micro_count, chips, block_rows(c, capacity), piece)

    def halves(c):
        return (CHUNK_PIECES[c], group, piece)

    def places(shape_of):
        return tuple(pltpu.VMEM(shape_of(c), jnp.int32) for c in range(CHUNKS))

    parts = micro_count * CHUNKS
    forward_out, backward_out = pl.pallas_call(
        functools.partial(relay_kernel, geometry),
        out_shape=(out, out),
        in_specs=[anywhere] * 2 + [inside] * 2 + [anywhere] * 3 + [inside],
        out_specs=(inside, inside),
        scratch_shapes=[
            pltpu.VMEM((width, hidden), bf16),
            pltpu.VMEM((width, hidden), bf16),
            pltpu.VMEM((hidden, width), bf16),
            pltpu.VMEM((micro_count, tokens, width), bf16),
            pltpu.VMEM((micro_count, tokens, width), bf16),
            per_chunk(lambda c: (rows_of(c), blocks_of(c))),
            per_chunk(lambda c: (blocks_of(c), rows_of(c))),
            pltpu.VMEM((group, chips * slots), bf16),
            places(lambda c: (micro_count, top_count, lanes_of(c))),
            places(lambda c: (micro_count, lanes_of(c), top_count)),
            pltpu.VMEM((micro_count, top_count, tokens), jnp.int32),
            per_chunk(exchange, 2),
            per_chunk(exchange, 2),
            per_chunk(exchange, 2),
            per_chunk(exchange, 2),
            per_chunk(exchange, 2),
            per_chunk(halves),
            per_chunk(halves),
            per_chunk(lambda c: (micro_count, *halves(c)), 2),
            pltpu.VMEM((micro_count, chips, slots, 128), f32),
            pltpu.VMEM((micro_count, 2, chips, slots, 128), f32),
            pltpu.VMEM((2, 2 * group, width), bf16),
            pltpu.VMEM((2 * group, 1), f32),
            pltpu.VMEM((micro_count, 2 * group, hidden), f32),
            pltpu.VMEM((micro_count, 2 * group, hidden), f32),
            pltpu.VMEM((2 * group, hidden), f32),
            pltpu.VMEM((micro_count, top_count, tokens, width), bf16),
            pltpu.VMEM((tokens, width), f32),
            pltpu.VMEM((micro_count, 8, tokens, 1), f32),
            dma((3,)),
            dma((parts,)),
            dma((parts,)),
            dma((2,)),
            dma((2, parts)),
            dma((2, parts)),
            dma,
            dma((2, parts)),
            dma((CHUNKS,)),
            dma((2, parts)),
            dma((2, parts)),
            dma((2, parts)),
            dma((micro_count, 2)),
            dma((micro_count, 2)),
        ],
        compiler_params=pltpu.CompilerParams(
            collective_id=0, has_side_effects=True, vmem_limit_bytes=66_000_000
        ),
    )(
        inputs,
        cotangent,
        norm_gain,
        router_weight[0].T,
        gate_weight[0],
        up_weight[0],
        down_weight[0],
        jnp.moveaxis(route_ids[0], 2, 1),
    )
    return (forward_out[None], backward_out[None])


def solution(mesh):
    return jax.shard_map(
        on_device,
        mesh=mesh,
        in_specs=(
            P(None, "expert", None),
            P(None, "expert", None),
            P("pipe", None),
            P("pipe", None, None),
            P("pipe", None, "expert"),
            P("pipe", None, "expert"),
            P("pipe", "expert", None),
            P("pipe", None, "expert", None),
        ),
        out_specs=(P("pipe", None, "expert", None), P("pipe", None, "expert", None)),
        check_vma=False,
    )
```

```python
import functools
import math

import jax
import jax.numpy as jnp
from jax import lax
from jax.experimental import pallas as pl
from jax.experimental.pallas import tpu as pltpu
from jax.sharding import PartitionSpec as P

EPSILON = 1e-06
CHUNK_PIECES = (8, 6)
CHUNKS = len(CHUNK_PIECES)
MESH = pl.DeviceIdType.MESH


def grid_of(chips):
    rows = math.isqrt(chips)
    while chips % rows:
        rows -= 1
    return rows, chips // rows


def block_rows(c, capacity):
    return -(-CHUNK_PIECES[c] * capacity // 8) * 8


def matmul(left, right):
    return jnp.dot(left, right, preferred_element_type=jnp.float32)


def matmul_t(left, right):
    return lax.dot_general(
        left, right, (((1,), (1,)), ((), ())), preferred_element_type=jnp.float32
    )


def relay_kernel(
    geometry,
    inputs_ref,
    cotangent_ref,
    gain_ref,
    router_ref,
    wg_hbm,
    wu_hbm,
    wd_hbm,
    ids_ref,
    out_ref,
    grad_ref,
    wg,
    wu,
    wd,
    acts,
    grads,
    unpack,
    repack,
    slot_pick,
    row_place,
    column_place,
    slot_place,
    dispatch_send,
    dispatch_recv,
    partner_rows,
    combine_send,
    combine_recv,
    half_send,
    half_own,
    half_recv,
    gate_send,
    gate_recv,
    rows_in,
    squares,
    gate_saved,
    up_saved,
    gate_rows,
    picked,
    kept,
    stats,
    weight_sem,
    act_sem,
    grad_sem,
    pipe_sem,
    dispatch_send_sem,
    dispatch_recv_sem,
    swap_send_sem,
    swap_recv_sem,
    half_send_sem,
    half_recv_sem,
    combine_send_sem,
    combine_recv_sem,
    gate_send_sem,
    gate_recv_sem,
):
    sections, micro_count, chips, capacity = geometry
    lines, columns = grid_of(chips)
    tokens, width = acts.shape[1], acts.shape[2]
    piece = width // sum(CHUNK_PIECES)
    group = chips * capacity
    slots = gate_send.shape[2]
    hidden = wg.shape[1]
    experts = router_ref.shape[0]
    bf16, f32 = jnp.bfloat16, jnp.float32
    section = lax.axis_index("pipe")
    place = lax.axis_index("expert")
    core = lax.rem(place, 2)
    chip = place // 2
    line, column = chip // columns, lax.rem(chip, columns)
    partner = chip * 2 + (1 - core)
    others = pl.ds(1, chips - 1)

    def peer(step, sign, to_core=core):
        to_line = lax.rem(line + sign * (step // columns) + lines, lines)
        to_column = lax.rem(column + sign * lax.rem(step, columns) + columns, columns)
        return {"expert": (to_line * columns + to_column) * 2 + to_core}

    def begin_of(c, q=0):
        return (sum(CHUNK_PIECES[:c]) + q) * piece

    def span(c):
        return slice(begin_of(c), begin_of(c + 1))

    def pieces_of(value):
        return [value[:, q : q + piece] for q in range(0, value.shape[1], piece)]

    def block_of(c):
        return block_rows(c, capacity)

    barrier = pltpu.get_barrier_semaphore()

    def greet(step, carry):
        for to_core in (core, 1 - core):
            pl.semaphore_signal(
                barrier, inc=1, device_id=peer(step, 1, to_core), device_id_type=MESH
            )
        return carry

    weights = [
        pltpu.make_async_copy(source, target, weight_sem.at[i])
        for i, (source, target) in enumerate([(wg_hbm, wg), (wu_hbm, wu), (wd_hbm, wd)])
    ]

    def fetch(source, target, semaphore):
        for m in range(micro_count):
            for c in range(CHUNKS):
                pltpu.make_async_copy(
                    source.at[m, :, span(c)],
                    target.at[m, :, span(c)],
                    semaphore.at[m * CHUNKS + c],
                ).start()

    @pl.when(section == 0)
    def _():
        fetch(inputs_ref, acts, act_sem)

    @pl.when(section == sections - 1)
    def _():
        fetch(cotangent_ref, grads, grad_sem)

    for copy in weights:
        copy.start()
    lax.fori_loop(1, chips, greet, 0)
    pl.semaphore_signal(barrier, inc=1, device_id={"expert": partner}, device_id_type=MESH)
    for sign in (1, sections - 1):
        pl.semaphore_signal(
            barrier,
            inc=1,
            device_id={"pipe": lax.rem(section + sign, sections)},
            device_id_type=MESH,
        )

    def iota(shape, axis):
        return lax.broadcasted_iota(jnp.int32, shape, axis)

    def hot(condition):
        return jnp.where(condition, 1.0, 0.0).astype(bf16)

    for c in range(CHUNKS):

        def place_of(number):
            within = lax.rem(number, block_of(c))
            q = within // capacity
            row = q * group + (number // block_of(c)) * capacity + lax.rem(within, capacity)
            return jnp.where(within < CHUNK_PIECES[c] * capacity, row, -1)

        shape = (CHUNK_PIECES[c] * group, chips * block_of(c))
        unpack[c][...] = hot(iota(shape, 0) == place_of(iota((1, shape[1]), 1)))
        repack[c][...] = hot(iota(shape[::-1], 1) == place_of(iota((shape[1], 1), 0)))
    shape = (group, chips * slots)
    wanted = iota((group, 1), 0)
    wanted = (wanted // capacity) * slots + lax.rem(wanted, capacity)
    slot_pick[...] = hot(iota(shape, 1) == wanted)

    earlier = hot(iota((tokens, tokens), 0) < iota((tokens, tokens), 1))
    for m in range(micro_count):
        ids = ids_ref[m]
        found = [hot(iota((experts, tokens), 0) == ids[k : k + 1]) for k in range(2)]
        counts = matmul(found[0] + found[1], earlier)
        ranks = [
            jnp.sum(counts * found[k].astype(f32), axis=0, keepdims=True) for k in range(2)
        ]
        ranks = jnp.concatenate(ranks, axis=0)
        to_line = lax.rem(ids // columns - line + lines, lines)
        to_column = lax.rem(lax.rem(ids, columns) - column + columns, columns)
        steps_to = (to_line * columns + to_column).astype(f32).astype(bf16)
        ranks_to = ranks.astype(bf16)
        for c in range(CHUNKS):
            lanes = CHUNK_PIECES[c] * tokens
            across = hot(iota((tokens, lanes), 0) == lax.rem(iota((1, lanes), 1), tokens))
            down = hot(lax.rem(iota((lanes, 1), 0), tokens) == iota((lanes, tokens), 1))
            where = matmul(steps_to, across).astype(jnp.int32) * block_of(c)
            where += matmul(ranks_to, across).astype(jnp.int32)
            row_place[c][m] = where + (iota((1, lanes), 1) // tokens) * capacity
            where = matmul_t(down, steps_to).astype(jnp.int32) * block_of(c)
            where += matmul_t(down, ranks_to).astype(jnp.int32)
            column_place[c][m] = where + (iota((lanes, 1), 0) // tokens) * capacity
        slot_place[m] = (steps_to.astype(f32) * slots + ranks).astype(jnp.int32)

    pl.semaphore_wait(barrier, 2 * (chips - 1) + 1 + 2)

    def wait_all(buffer, semaphore):
        pltpu.make_async_copy(buffer, buffer, semaphore).wait()

    def post(values, m, c, send, recv, send_sem, recv_sem, sign):
        values = values.astype(bf16).reshape(chips, block_of(c), piece)
        recv[m, 0] = values[0]
        send[m, others] = values[1:]

        def start(step, carry):
            pltpu.make_async_remote_copy(
                src_ref=send.at[m, step],
                dst_ref=recv.at[m, step],
                send_sem=send_sem.at[m * CHUNKS + c],
                recv_sem=recv_sem.at[m * CHUNKS + c],
                device_id=peer(step, sign),
                device_id_type=MESH,
            ).start()
            return carry

        lax.fori_loop(1, chips, start, 0)

    def dispatch(stacked, m, c, way):
        target = row_place[c][m]
        rows = iota((chips * block_of(c), target.shape[1]), 0)
        table = hot(rows == target[0:1]) + hot(rows == target[1:2])
        post(
            matmul(table, stacked),
            m,
            c,
            dispatch_send[way][c],
            dispatch_recv[way][c],
            dispatch_send_sem.at[way],
            dispatch_recv_sem.at[way],
            1,
        )

    def expert_hot(m):
        same = hot(iota((tokens, tokens), 0) == iota((tokens, tokens), 1))
        names = matmul_t(same, ids_ref[m].astype(f32).astype(bf16)).astype(jnp.int32)
        return [
            jnp.where(iota((tokens, experts), 1) == names[:, k : k + 1], 1.0, 0.0)
            for k in range(2)
        ]

    def unpack_rows(source, m, c, way, part):
        rows = matmul(unpack[c][...], source[m].reshape(chips * block_of(c), piece))
        mine = slice(part * group, (part + 1) * group)
        square = jnp.zeros((group, piece), f32)
        for q in range(CHUNK_PIECES[c]):
            at = slice(begin_of(c, q), begin_of(c, q + 1))
            found = rows[q * group : (q + 1) * group]
            if way == 0:
                square += found * found
                found = found * gain_ref[:, at]
            rows_in[way, mine, at] = found.astype(bf16)
        if way == 0:
            square = jnp.sum(square, axis=1, keepdims=True)
            squares[mine] = square if c == 0 else squares[mine] + square

    def take_rows(m, way, meanwhile, product):
        swaps = []
        for c in range(CHUNKS):
            number = m * CHUNKS + c
            send, recv = dispatch_send[way][c], dispatch_recv[way][c]
            wait_all(recv.at[m, others], dispatch_recv_sem.at[way, number])
            swap = pltpu.make_async_remote_copy(
                src_ref=recv.at[m],
                dst_ref=partner_rows[way][c].at[m],
                send_sem=swap_send_sem.at[c],
                recv_sem=swap_recv_sem.at[way, number],
                device_id={"expert": partner},
                device_id_type=MESH,
            )
            swap.start()
            swaps.append(swap)
            wait_all(send.at[m, others], dispatch_send_sem.at[way, number])
            unpack_rows(recv, m, c, way, 0)
        meanwhile()
        total = None
        for c in range(CHUNKS):
            swaps[c].wait()
            unpack_rows(partner_rows[way][c], m, c, way, 1)
            found = product(c)
            total = found if total is None else [a + b for a, b in zip(total, found)]
        return total

    def halves_and_combine(m, way, product):
        copies = []
        for c in range(CHUNKS):
            part = product(c).astype(bf16)
            for q, values in enumerate(pieces_of(part)):
                half_own[c][q] = values[:group]
                half_send[c][q] = values[group:]
            copy = pltpu.make_async_remote_copy(
                src_ref=half_send[c],
                dst_ref=half_recv[way][c].at[m],
                send_sem=half_send_sem.at[c],
                recv_sem=half_recv_sem.at[way, m * CHUNKS + c],
                device_id={"expert": partner},
                device_id_type=MESH,
            )
            copy.start()
            copies.append(copy)
        for c in range(CHUNKS):
            copies[c].wait()
            total = half_own[c][...].astype(f32) + half_recv[way][c][m].astype(f32)
            total = total.astype(bf16).reshape(CHUNK_PIECES[c] * group, piece)
            post(
                matmul(repack[c][...], total),
                m,
                c,
                combine_send[way][c],
                combine_recv[way][c],
                combine_send_sem.at[way],
                combine_recv_sem.at[way],
                -1,
            )

    def send_gates(m, gates):
        target = slot_place[m]
        rows = iota((chips * slots, tokens), 0)
        tables = [hot(rows == target[k : k + 1]) for k in range(2)]
        spread = jnp.zeros((chips * slots, 128), f32)
        for k in range(2):
            value = jnp.broadcast_to(gates[k], (tokens, 128))
            high = value.astype(bf16)
            low = (value - high.astype(f32)).astype(bf16)
            spread += matmul(tables[k], high) + matmul(tables[k], low)
        spread = spread.reshape(chips, slots, 128)
        gate_send[m] = spread
        gate_recv[m, 0, 0] = spread[0]

        def copy_to(step, part):
            pltpu.make_async_remote_copy(
                src_ref=gate_send.at[m, step],
                dst_ref=gate_recv.at[m, part, step],
                send_sem=gate_send_sem.at[m, part],
                recv_sem=gate_recv_sem.at[m, part],
                device_id=peer(step, 1, core if part == 0 else 1 - core),
                device_id_type=MESH,
            ).start()

        def start(step, carry):
            copy_to(step, 0)
            copy_to(step, 1)
            return carry

        copy_to(0, 1)
        lax.fori_loop(1, chips, start, 0)

    def take_gates(m):
        gates = []
        for part, arrived in enumerate((others, pl.ds(0, chips))):
            wait_all(gate_recv.at[m, part, arrived], gate_recv_sem.at[m, part])
            wait_all(gate_send.at[m, arrived], gate_send_sem.at[m, part])
            value = gate_recv[m, part].reshape(chips * slots, 128)
            high = value.astype(bf16)
            low = (value - high.astype(f32)).astype(bf16)
            gates.append(matmul(slot_pick[...], high) + matmul(slot_pick[...], low))
        return jnp.concatenate(gates, axis=0)[:, :1]

    def forward_send(m, c):
        wait_all(acts.at[m, :, span(c)], act_sem.at[m * CHUNKS + c])
        dispatch(jnp.concatenate(pieces_of(acts[m, :, span(c)]), axis=0), m, c, 0)
        if c < CHUNKS - 1:
            return
        wide_in = acts[m].astype(f32)
        scale = lax.rsqrt(jnp.mean(wide_in * wide_in, axis=1, keepdims=True) + EPSILON)
        normed = (wide_in * scale * gain_ref[...]).astype(bf16)
        logits = matmul_t(normed, router_ref[...])
        chances = [
            1.0 / (1.0 + jnp.exp(-jnp.sum(logits * named, axis=1, keepdims=True)))
            for named in expert_hot(m)
        ]
        total = chances[0] + chances[1]
        gates = [chance / total for chance in chances]
        send_gates(m, gates)
        stats[m, 0] = scale
        for k in range(2):
            stats[m, 1 + k] = chances[k]
            stats[m, 3 + k] = gates[k]

    def forward_expert(m):
        @pl.when(m == 0)
        def _():
            for copy in weights:
                copy.wait()

        def product(c):
            rows = rows_in[0, :, span(c)]
            return [matmul(rows, wg[span(c)]), matmul(rows, wu[span(c)])]

        gate_pre, up_pre = take_rows(m, 0, lambda: None, product)
        scale = lax.rsqrt(squares[...] / width + EPSILON)
        gate_pre = gate_pre * scale
        up_pre = up_pre * scale
        gate_saved[m] = gate_pre
        up_saved[m] = up_pre
        inner = (gate_pre / (1.0 + jnp.exp(-gate_pre)) * up_pre).astype(bf16)
        halves_and_combine(m, 0, lambda d: matmul(inner, wd[:, span(d)]))

    def receive_combined(m, c, way):
        number = m * CHUNKS + c
        recv = combine_recv[way][c]
        wait_all(recv.at[m, others], combine_recv_sem.at[way, number])
        wait_all(combine_send[way][c].at[m, others], combine_send_sem.at[way, number])
        return recv[m].reshape(chips * block_of(c), piece)

    def column_tables(m, c):
        target = column_place[c][m]
        places = iota((target.shape[0], chips * block_of(c)), 1)
        return [hot(places == target[:, k : k + 1]) for k in range(2)]

    def forward_finish(m, c):
        received = receive_combined(m, c, 0)
        found = [matmul(table, received) for table in column_tables(m, c)]
        for q in range(CHUNK_PIECES[c]):
            at = slice(begin_of(c, q), begin_of(c, q + 1))
            total = acts[m, :, at].astype(f32)
            for k in range(2):
                rows = found[k][q * tokens : (q + 1) * tokens]
                picked[m, k, :, at] = rows.astype(bf16)
                total += stats[m, 3 + k] * rows
            out_ref[m, :, at] = total.astype(bf16)

        @pl.when(section < sections - 1)
        def _():
            pltpu.make_async_remote_copy(
                src_ref=out_ref.at[m, :, span(c)],
                dst_ref=acts.at[m, :, span(c)],
                send_sem=pipe_sem.at[0],
                recv_sem=act_sem.at[m * CHUNKS + c],
                device_id={"pipe": section + 1},
                device_id_type=MESH,
            ).start()

    def backward_send(m, c):
        wait_all(grads.at[m, :, span(c)], grad_sem.at[m * CHUNKS + c])
        dispatch(jnp.concatenate(pieces_of(grads[m, :, span(c)]), axis=0), m, c, 1)

    def backward_expert(m):
        def load_gates():
            gate_rows[...] = take_gates(m)

        (inner_grad,) = take_rows(
            m, 1, load_gates, lambda c: [matmul_t(rows_in[1, :, span(c)], wd[:, span(c)])]
        )
        inner_grad = inner_grad * gate_rows[...]
        gate_pre = gate_saved[m]
        sigmoid = 1.0 / (1.0 + jnp.exp(-gate_pre))
        pre_grad = (
            inner_grad * up_saved[m] * sigmoid * (1.0 + gate_pre * (1.0 - sigmoid))
        ).astype(bf16)
        up_grad = (inner_grad * gate_pre * sigmoid).astype(bf16)
        halves_and_combine(
            m, 1, lambda d: matmul_t(pre_grad, wg[span(d)]) + matmul_t(up_grad, wu[span(d)])
        )

    def score_slopes(m):
        upstream = grads[m].astype(f32)
        slopes = [
            jnp.sum(upstream * picked[m, k].astype(f32), axis=1, keepdims=True)
            for k in range(2)
        ]
        weighted = stats[m, 3] * slopes[0] + stats[m, 4] * slopes[1]
        total = stats[m, 1] + stats[m, 2]
        for k in range(2):
            chance = stats[m, 1 + k]
            stats[m, 5 + k] = (slopes[k] - weighted) / total * chance * (1.0 - chance)

    def backward_finish(m, c):
        if c == 0:
            score_slopes(m)
        named = expert_hot(m)
        router_table = (stats[m, 5] * named[0] + stats[m, 6] * named[1]).astype(bf16)
        routed = matmul(router_table, router_ref[:, span(c)])
        received = receive_combined(m, c, 1)
        tables = column_tables(m, c)
        summed = matmul(tables[0] + tables[1], received)
        inner = jnp.zeros((tokens, piece), f32)
        for q in range(CHUNK_PIECES[c]):
            at = slice(begin_of(c, q), begin_of(c, q + 1))
            near = slice(q * piece, (q + 1) * piece)
            normed_grad = summed[q * tokens : (q + 1) * tokens] + routed[:, near]
            normed_grad = normed_grad * gain_ref[:, at]
            inner += acts[m, :, at].astype(f32) * normed_grad
            kept[:, at] = normed_grad
        inner = jnp.sum(inner, axis=1, keepdims=True)
        if c > 0:
            inner += stats[m, 7]
        if c < CHUNKS - 1:
            stats[m, 7] = inner
            return
        scale = stats[m, 0]
        inner = scale * scale * scale * (inner / width)
        for d in range(CHUNKS):
            result = grads[m, :, span(d)].astype(f32) + scale * kept[:, span(d)]
            result -= acts[m, :, span(d)].astype(f32) * inner
            grad_ref[m, :, span(d)] = result.astype(bf16)

            @pl.when(section > 0)
            def _():
                pltpu.make_async_remote_copy(
                    src_ref=grad_ref.at[m, :, span(d)],
                    dst_ref=grads.at[m, :, span(d)],
                    send_sem=pipe_sem.at[1],
                    recv_sem=grad_sem.at[m * CHUNKS + d],
                    device_id={"pipe": section - 1},
                    device_id_type=MESH,
                ).start()

    steps = (
        forward_send,
        forward_expert,
        forward_finish,
        backward_send,
        backward_expert,
        backward_finish,
    )
    words = order_words(sections, micro_count)

    def run(i, carry):
        word, *counts = carry
        for w in range(len(words[0])):
            fresh = jnp.int32(0)
            for s, row in enumerate(words):
                fresh += jnp.where(section == s, row[w], 0)
            word = jnp.where(i == w * DIGITS, fresh, word)
        kind = lax.rem(word, 8)
        for number, step in enumerate(steps):
            if number in WHOLE:

                @pl.when(kind == number)
                def _():
                    step(counts[number])

                continue
            m, c = counts[number] // CHUNKS, lax.rem(counts[number], CHUNKS)
            for d in range(CHUNKS):

                @pl.when((kind == number) & (c == d))
                def _():
                    step(m, d)

        counts = [count + jnp.where(kind == n, 1, 0) for n, count in enumerate(counts)]
        return (word // 8, *counts)

    total_steps = micro_count * (4 * CHUNKS + 2)
    lax.fori_loop(0, total_steps, run, (jnp.int32(0),) * 7)

    @pl.when(section < sections - 1)
    def _():
        wait_all(out_ref, pipe_sem.at[0])

    @pl.when(section > 0)
    def _():
        wait_all(grad_ref, pipe_sem.at[1])


KINDS = "abcABC"
WHOLE = (1, 4)
DIGITS = 10
ORDERS = (
    "aaabcacabcacbccaabccAABAACBAACBCACACCBCC",
    "aabacacbaaccbccaabccAABCACABCAACBAACCBCC",
    "aabcacabaaccbcacAAaBbCCAAccBAACCBCAACBCC",
    "AAAAAaabBacacCAACbaaBccbCCBccaCaCAbBccCC",
)


def order_words(sections, micro_count):
    orders = ORDERS
    if (sections, micro_count) != (4, 4):
        orders = ("aabcc" * micro_count + "AABCC" * micro_count,) * (sections - 1)
        orders += ("AA" * micro_count + "aabcc" * micro_count + "BCC" * micro_count,)
    words = []
    for order in orders:
        row = []
        for begin in range(0, len(order), DIGITS):
            digits = [KINDS.index(kind) for kind in order[begin : begin + DIGITS]]
            row.append(sum(digit * 8**j for j, digit in enumerate(digits)))
        words.append(row)
    return words


def on_device(
    inputs, cotangent, norm_gain, router_weight, gate_weight, up_weight, down_weight, route_ids
):
    sections = lax.axis_size("pipe")
    chips = lax.axis_size("expert") // 2
    micro_count, tokens, width = inputs.shape
    experts = router_weight.shape[2]
    top_count = route_ids.shape[3]
    capacity = min(tokens, (5 * tokens * top_count + 4 * experts - 1) // (4 * experts))
    hidden = gate_weight.shape[2]
    piece = width // sum(CHUNK_PIECES)
    group = chips * capacity
    slots = -(-capacity // 8) * 8
    anywhere = pl.BlockSpec(memory_space=pl.ANY)
    inside = pl.BlockSpec(memory_space=pltpu.VMEM)
    bf16, f32 = jnp.bfloat16, jnp.float32
    out = jax.ShapeDtypeStruct((micro_count, tokens, width), bf16)
    dma = pltpu.SemaphoreType.DMA
    geometry = (sections, micro_count, chips, capacity)

    def per_chunk(shape_of, ways=0):
        chunks = tuple(pltpu.VMEM(shape_of(c), bf16) for c in range(CHUNKS))
        return (chunks, chunks) if ways else chunks

    def rows_of(c):
        return CHUNK_PIECES[c] * group

    def blocks_of(c):
        return chips * block_rows(c, capacity)

    def lanes_of(c):
        return CHUNK_PIECES[c] * tokens

    def exchange(c):
        return (micro_count, chips, block_rows(c, capacity), piece)

    def halves(c):
        return (CHUNK_PIECES[c], group, piece)

    def places(shape_of):
        return tuple(pltpu.VMEM(shape_of(c), jnp.int32) for c in range(CHUNKS))

    parts = micro_count * CHUNKS
    forward_out, backward_out = pl.pallas_call(
        functools.partial(relay_kernel, geometry),
        out_shape=(out, out),
        in_specs=[anywhere] * 2 + [inside] * 2 + [anywhere] * 3 + [inside],
        out_specs=(inside, inside),
        scratch_shapes=[
            pltpu.VMEM((width, hidden), bf16),
            pltpu.VMEM((width, hidden), bf16),
            pltpu.VMEM((hidden, width), bf16),
            pltpu.VMEM((micro_count, tokens, width), bf16),
            pltpu.VMEM((micro_count, tokens, width), bf16),
            per_chunk(lambda c: (rows_of(c), blocks_of(c))),
            per_chunk(lambda c: (blocks_of(c), rows_of(c))),
            pltpu.VMEM((group, chips * slots), bf16),
            places(lambda c: (micro_count, top_count, lanes_of(c))),
            places(lambda c: (micro_count, lanes_of(c), top_count)),
            pltpu.VMEM((micro_count, top_count, tokens), jnp.int32),
            per_chunk(exchange, 2),
            per_chunk(exchange, 2),
            per_chunk(exchange, 2),
            per_chunk(exchange, 2),
            per_chunk(exchange, 2),
            per_chunk(halves),
            per_chunk(halves),
            per_chunk(lambda c: (micro_count, *halves(c)), 2),
            pltpu.VMEM((micro_count, chips, slots, 128), f32),
            pltpu.VMEM((micro_count, 2, chips, slots, 128), f32),
            pltpu.VMEM((2, 2 * group, width), bf16),
            pltpu.VMEM((2 * group, 1), f32),
            pltpu.VMEM((micro_count, 2 * group, hidden), f32),
            pltpu.VMEM((micro_count, 2 * group, hidden), f32),
            pltpu.VMEM((2 * group, 1), f32),
            pltpu.VMEM((micro_count, top_count, tokens, width), bf16),
            pltpu.VMEM((tokens, width), f32),
            pltpu.VMEM((micro_count, 8, tokens, 1), f32),
            dma((3,)),
            dma((parts,)),
            dma((parts,)),
            dma((2,)),
            dma((2, parts)),
            dma((2, parts)),
            dma((CHUNKS,)),
            dma((2, parts)),
            dma((CHUNKS,)),
            dma((2, parts)),
            dma((2, parts)),
            dma((2, parts)),
            dma((micro_count, 2)),
            dma((micro_count, 2)),
        ],
        compiler_params=pltpu.CompilerParams(
            collective_id=0, has_side_effects=True, vmem_limit_bytes=66_000_000
        ),
    )(
        inputs,
        cotangent,
        norm_gain,
        router_weight[0].T,
        gate_weight[0],
        up_weight[0],
        down_weight[0],
        jnp.moveaxis(route_ids[0], 2, 1),
    )
    return (forward_out[None], backward_out[None])


def solution(mesh):
    return jax.shard_map(
        on_device,
        mesh=mesh,
        in_specs=(
            P(None, "expert", None),
            P(None, "expert", None),
            P("pipe", None),
            P("pipe", None, None),
            P("pipe", None, "expert"),
            P("pipe", None, "expert"),
            P("pipe", "expert", None),
            P("pipe", None, "expert", None),
        ),
        out_specs=(P("pipe", None, "expert", None), P("pipe", None, "expert", None)),
        check_vma=False,
    )
```

```python
import functools
import math

import jax
import jax.numpy as jnp
from jax import lax
from jax.experimental import pallas as pl
from jax.experimental.pallas import tpu as pltpu
from jax.sharding import PartitionSpec as P

EPSILON = 1e-06
CHUNK_PIECES = (8, 6)
CHUNKS = len(CHUNK_PIECES)
MESH = pl.DeviceIdType.MESH


def grid_of(chips):
    rows = math.isqrt(chips)
    while chips % rows:
        rows -= 1
    return rows, chips // rows


def block_rows(c, capacity):
    return -(-CHUNK_PIECES[c] * capacity // 8) * 8


def matmul(left, right):
    return jnp.dot(left, right, preferred_element_type=jnp.float32)


def matmul_t(left, right):
    return lax.dot_general(
        left, right, (((1,), (1,)), ((), ())), preferred_element_type=jnp.float32
    )


def relay_kernel(
    geometry,
    inputs_ref,
    cotangent_ref,
    gain_ref,
    router_ref,
    wg_hbm,
    wu_hbm,
    wd_hbm,
    ids_ref,
    out_ref,
    grad_ref,
    wg,
    wu,
    wd,
    acts,
    grads,
    unpack,
    repack,
    slot_pick,
    row_place,
    column_place,
    slot_place,
    dispatch_send,
    dispatch_recv,
    partner_rows,
    combine_send,
    combine_recv,
    half_send,
    half_own,
    half_recv,
    gate_send,
    gate_recv,
    rows_in,
    squares,
    gate_saved,
    up_saved,
    gate_rows,
    picked,
    kept,
    stats,
    weight_sem,
    act_sem,
    grad_sem,
    pipe_sem,
    dispatch_send_sem,
    dispatch_recv_sem,
    swap_send_sem,
    swap_recv_sem,
    half_send_sem,
    half_recv_sem,
    combine_send_sem,
    combine_recv_sem,
    gate_send_sem,
    gate_recv_sem,
):
    sections, micro_count, chips, capacity = geometry
    lines, columns = grid_of(chips)
    tokens, width = acts.shape[1], acts.shape[2]
    piece = width // sum(CHUNK_PIECES)
    group = chips * capacity
    half_group, half_chips = group // 2, chips // 2
    slots = gate_send.shape[2]
    hidden = wg.shape[1]
    experts = router_ref.shape[0]
    bf16, f32 = jnp.bfloat16, jnp.float32
    section = lax.axis_index("pipe")
    place = lax.axis_index("expert")
    core = lax.rem(place, 2)
    chip = place // 2
    line, column = chip // columns, lax.rem(chip, columns)
    partner = chip * 2 + (1 - core)
    others = pl.ds(1, chips - 1)

    def peer(step, sign, to_core=core):
        to_line = lax.rem(line + sign * (step // columns) + lines, lines)
        to_column = lax.rem(column + sign * lax.rem(step, columns) + columns, columns)
        return {"expert": (to_line * columns + to_column) * 2 + to_core}

    def begin_of(c, q=0):
        return (sum(CHUNK_PIECES[:c]) + q) * piece

    def span(c):
        return slice(begin_of(c), begin_of(c + 1))

    def pieces_of(value):
        return [value[:, q : q + piece] for q in range(0, value.shape[1], piece)]

    def block_of(c):
        return block_rows(c, capacity)

    barrier = pltpu.get_barrier_semaphore()

    def greet(step, carry):
        for to_core in (core, 1 - core):
            pl.semaphore_signal(
                barrier, inc=1, device_id=peer(step, 1, to_core), device_id_type=MESH
            )
        return carry

    weights = [
        pltpu.make_async_copy(source, target, weight_sem.at[i])
        for i, (source, target) in enumerate([(wg_hbm, wg), (wu_hbm, wu), (wd_hbm, wd)])
    ]

    def fetch(source, target, semaphore):
        for m in range(micro_count):
            for c in range(CHUNKS):
                pltpu.make_async_copy(
                    source.at[m, :, span(c)],
                    target.at[m, :, span(c)],
                    semaphore.at[m * CHUNKS + c],
                ).start()

    @pl.when(section == 0)
    def _():
        fetch(inputs_ref, acts, act_sem)

    @pl.when(section == sections - 1)
    def _():
        fetch(cotangent_ref, grads, grad_sem)

    for copy in weights:
        copy.start()
    lax.fori_loop(1, chips, greet, 0)
    pl.semaphore_signal(barrier, inc=1, device_id={"expert": partner}, device_id_type=MESH)
    for sign in (1, sections - 1):
        pl.semaphore_signal(
            barrier,
            inc=1,
            device_id={"pipe": lax.rem(section + sign, sections)},
            device_id_type=MESH,
        )

    def iota(shape, axis):
        return lax.broadcasted_iota(jnp.int32, shape, axis)

    def hot(condition):
        return jnp.where(condition, 1.0, 0.0).astype(bf16)

    earlier = hot(iota((tokens, tokens), 0) < iota((tokens, tokens), 1))
    for m in range(micro_count):
        ids = ids_ref[m]
        found = [hot(iota((experts, tokens), 0) == ids[k : k + 1]) for k in range(2)]
        counts = matmul(found[0] + found[1], earlier)
        ranks = [
            jnp.sum(counts * found[k].astype(f32), axis=0, keepdims=True) for k in range(2)
        ]
        ranks = jnp.concatenate(ranks, axis=0)
        to_line = lax.rem(ids // columns - line + lines, lines)
        to_column = lax.rem(lax.rem(ids, columns) - column + columns, columns)
        steps_to = (to_line * columns + to_column).astype(f32).astype(bf16)
        ranks_to = ranks.astype(bf16)
        for c in range(CHUNKS):
            lanes = CHUNK_PIECES[c] * tokens
            across = hot(iota((tokens, lanes), 0) == lax.rem(iota((1, lanes), 1), tokens))
            down = hot(lax.rem(iota((lanes, 1), 0), tokens) == iota((lanes, tokens), 1))
            where = matmul(steps_to, across).astype(jnp.int32) * block_of(c)
            where += matmul(ranks_to, across).astype(jnp.int32)
            row_place[c][m] = where + (iota((1, lanes), 1) // tokens) * capacity
            where = matmul_t(down, steps_to).astype(jnp.int32) * block_of(c)
            where += matmul_t(down, ranks_to).astype(jnp.int32)
            column_place[c][m] = where + (iota((lanes, 1), 0) // tokens) * capacity
        slot_place[m] = (steps_to.astype(f32) * slots + ranks).astype(jnp.int32)

    pl.semaphore_wait(barrier, 2 * (chips - 1) + 1 + 2)

    def build_matrices():
        for c in range(CHUNKS):

            def place_of(number):
                within = lax.rem(number, block_of(c))
                q = within // capacity
                row = q * half_group + (number // block_of(c)) * capacity + lax.rem(within, capacity)
                return jnp.where(within < CHUNK_PIECES[c] * capacity, row, -1)

            shape = (CHUNK_PIECES[c] * half_group, half_chips * block_of(c))
            unpack[c][...] = hot(iota(shape, 0) == place_of(iota((1, shape[1]), 1)))
            repack[c][...] = hot(iota(shape[::-1], 1) == place_of(iota((shape[1], 1), 0)))
        shape = (group, chips * slots)
        wanted = iota((group, 1), 0)
        wanted = (wanted // capacity) * slots + lax.rem(wanted, capacity)
        slot_pick[...] = hot(iota(shape, 1) == wanted)

    def wait_all(buffer, semaphore):
        pltpu.make_async_copy(buffer, buffer, semaphore).wait()

    def post(values, m, c, send, recv, send_sem, recv_sem, sign):
        values = values.astype(bf16).reshape(chips, block_of(c), piece)
        recv[m, 0] = values[0]
        send[m, others] = values[1:]

        def start(step, carry):
            pltpu.make_async_remote_copy(
                src_ref=send.at[m, step],
                dst_ref=recv.at[m, step],
                send_sem=send_sem.at[m * CHUNKS + c],
                recv_sem=recv_sem.at[m * CHUNKS + c],
                device_id=peer(step, sign),
                device_id_type=MESH,
            ).start()
            return carry

        lax.fori_loop(1, chips, start, 0)

    def dispatch(stacked, m, c, way):
        target = row_place[c][m]
        rows = iota((chips * block_of(c), target.shape[1]), 0)
        table = hot(rows == target[0:1]) + hot(rows == target[1:2])
        post(
            matmul(table, stacked),
            m,
            c,
            dispatch_send[way][c],
            dispatch_recv[way][c],
            dispatch_send_sem.at[way],
            dispatch_recv_sem.at[way],
            1,
        )

    def expert_hot(m):
        same = hot(iota((tokens, tokens), 0) == iota((tokens, tokens), 1))
        names = matmul_t(same, ids_ref[m].astype(f32).astype(bf16)).astype(jnp.int32)
        return [
            jnp.where(iota((tokens, experts), 1) == names[:, k : k + 1], 1.0, 0.0)
            for k in range(2)
        ]

    def unpack_rows(source, m, c, way, part):
        rows = [
            matmul(unpack[c][...], blocks.reshape(half_chips * block_of(c), piece))
            for blocks in (source[m, :half_chips], source[m, half_chips:])
        ]
        mine = slice(part * group, (part + 1) * group)
        square = jnp.zeros((group, piece), f32)
        for q in range(CHUNK_PIECES[c]):
            at = slice(begin_of(c, q), begin_of(c, q + 1))
            found = [half[q * half_group : (q + 1) * half_group] for half in rows]
            found = jnp.concatenate(found, axis=0)
            if way == 0:
                square += found * found
                found = found * gain_ref[:, at]
            rows_in[way, mine, at] = found.astype(bf16)
        if way == 0:
            square = jnp.sum(square, axis=1, keepdims=True)
            squares[mine] = square if c == 0 else squares[mine] + square

    def take_rows(m, way, meanwhile, product):
        swaps = []
        for c in range(CHUNKS):
            number = m * CHUNKS + c
            send, recv = dispatch_send[way][c], dispatch_recv[way][c]
            wait_all(recv.at[m, others], dispatch_recv_sem.at[way, number])
            swap = pltpu.make_async_remote_copy(
                src_ref=recv.at[m],
                dst_ref=partner_rows[way][c].at[m],
                send_sem=swap_send_sem.at[c],
                recv_sem=swap_recv_sem.at[way, number],
                device_id={"expert": partner},
                device_id_type=MESH,
            )
            swap.start()
            swaps.append(swap)
            wait_all(send.at[m, others], dispatch_send_sem.at[way, number])
            unpack_rows(recv, m, c, way, 0)
        meanwhile()
        total = None
        for c in range(CHUNKS):
            swaps[c].wait()
            unpack_rows(partner_rows[way][c], m, c, way, 1)
            found = product(c)
            total = found if total is None else [a + b for a, b in zip(total, found)]
        return total

    def halves_and_combine(m, way, product):
        copies = []
        for c in range(CHUNKS):
            part = product(c).astype(bf16)
            for q, values in enumerate(pieces_of(part)):
                half_own[c][q] = values[:group]
                half_send[c][q] = values[group:]
            copy = pltpu.make_async_remote_copy(
                src_ref=half_send[c],
                dst_ref=half_recv[way][c].at[m],
                send_sem=half_send_sem.at[c],
                recv_sem=half_recv_sem.at[way, m * CHUNKS + c],
                device_id={"expert": partner},
                device_id_type=MESH,
            )
            copy.start()
            copies.append(copy)
        for c in range(CHUNKS):
            copies[c].wait()
            total = half_own[c][...].astype(f32) + half_recv[way][c][m].astype(f32)
            packed = [
                matmul(
                    repack[c][...],
                    half.reshape(CHUNK_PIECES[c] * half_group, piece).astype(bf16),
                )
                for half in (total[:, :half_group], total[:, half_group:])
            ]
            post(
                jnp.concatenate(packed, axis=0),
                m,
                c,
                combine_send[way][c],
                combine_recv[way][c],
                combine_send_sem.at[way],
                combine_recv_sem.at[way],
                -1,
            )

    def send_gates(m, gates):
        target = slot_place[m]
        rows = iota((chips * slots, tokens), 0)
        tables = [hot(rows == target[k : k + 1]) for k in range(2)]
        spread = jnp.zeros((chips * slots, 128), f32)
        for k in range(2):
            value = jnp.broadcast_to(gates[k], (tokens, 128))
            high = value.astype(bf16)
            low = (value - high.astype(f32)).astype(bf16)
            spread += matmul(tables[k], high) + matmul(tables[k], low)
        spread = spread.reshape(chips, slots, 128)
        gate_send[m] = spread
        gate_recv[m, 0, 0] = spread[0]

        def copy_to(step, part):
            pltpu.make_async_remote_copy(
                src_ref=gate_send.at[m, step],
                dst_ref=gate_recv.at[m, part, step],
                send_sem=gate_send_sem.at[m, part],
                recv_sem=gate_recv_sem.at[m, part],
                device_id=peer(step, 1, core if part == 0 else 1 - core),
                device_id_type=MESH,
            ).start()

        def start(step, carry):
            copy_to(step, 0)
            copy_to(step, 1)
            return carry

        copy_to(0, 1)
        lax.fori_loop(1, chips, start, 0)

    def take_gates(m):
        gates = []
        for part, arrived in enumerate((others, pl.ds(0, chips))):
            wait_all(gate_recv.at[m, part, arrived], gate_recv_sem.at[m, part])
            wait_all(gate_send.at[m, arrived], gate_send_sem.at[m, part])
            value = gate_recv[m, part].reshape(chips * slots, 128)
            high = value.astype(bf16)
            low = (value - high.astype(f32)).astype(bf16)
            gates.append(matmul(slot_pick[...], high) + matmul(slot_pick[...], low))
        return jnp.concatenate(gates, axis=0)[:, :1]

    def forward_send(m, c):
        wait_all(acts.at[m, :, span(c)], act_sem.at[m * CHUNKS + c])
        dispatch(jnp.concatenate(pieces_of(acts[m, :, span(c)]), axis=0), m, c, 0)
        if c < CHUNKS - 1:
            return
        wide_in = acts[m].astype(f32)
        scale = lax.rsqrt(jnp.mean(wide_in * wide_in, axis=1, keepdims=True) + EPSILON)
        normed = (wide_in * scale * gain_ref[...]).astype(bf16)
        logits = matmul_t(normed, router_ref[...])
        chances = [
            1.0 / (1.0 + jnp.exp(-jnp.sum(logits * named, axis=1, keepdims=True)))
            for named in expert_hot(m)
        ]
        total = chances[0] + chances[1]
        gates = [chance / total for chance in chances]
        send_gates(m, gates)
        stats[m, 0] = scale
        for k in range(2):
            stats[m, 1 + k] = chances[k]
            stats[m, 3 + k] = gates[k]

    def forward_expert(m):
        @pl.when(m == 0)
        def _():
            build_matrices()
            for copy in weights:
                copy.wait()

        def product(c):
            rows = rows_in[0, :, span(c)]
            return [matmul(rows, wg[span(c)]), matmul(rows, wu[span(c)])]

        gate_pre, up_pre = take_rows(m, 0, lambda: None, product)
        scale = lax.rsqrt(squares[...] / width + EPSILON)
        gate_pre = gate_pre * scale
        up_pre = up_pre * scale
        gate_saved[m] = gate_pre
        up_saved[m] = up_pre
        inner = (gate_pre / (1.0 + jnp.exp(-gate_pre)) * up_pre).astype(bf16)
        halves_and_combine(m, 0, lambda d: matmul(inner, wd[:, span(d)]))

    def receive_combined(m, c, way):
        number = m * CHUNKS + c
        recv = combine_recv[way][c]
        wait_all(recv.at[m, others], combine_recv_sem.at[way, number])
        wait_all(combine_send[way][c].at[m, others], combine_send_sem.at[way, number])
        return recv[m].reshape(chips * block_of(c), piece)

    def column_tables(m, c):
        target = column_place[c][m]
        places = iota((target.shape[0], chips * block_of(c)), 1)
        return [hot(places == target[:, k : k + 1]) for k in range(2)]

    def forward_finish(m, c):
        received = receive_combined(m, c, 0)
        found = [matmul(table, received) for table in column_tables(m, c)]
        for q in range(CHUNK_PIECES[c]):
            at = slice(begin_of(c, q), begin_of(c, q + 1))
            total = acts[m, :, at].astype(f32)
            for k in range(2):
                rows = found[k][q * tokens : (q + 1) * tokens]
                picked[m, k, :, at] = rows.astype(bf16)
                total += stats[m, 3 + k] * rows
            out_ref[m, :, at] = total.astype(bf16)

        @pl.when(section < sections - 1)
        def _():
            pltpu.make_async_remote_copy(
                src_ref=out_ref.at[m, :, span(c)],
                dst_ref=acts.at[m, :, span(c)],
                send_sem=pipe_sem.at[0],
                recv_sem=act_sem.at[m * CHUNKS + c],
                device_id={"pipe": section + 1},
                device_id_type=MESH,
            ).start()

    def backward_send(m, c):
        wait_all(grads.at[m, :, span(c)], grad_sem.at[m * CHUNKS + c])
        dispatch(jnp.concatenate(pieces_of(grads[m, :, span(c)]), axis=0), m, c, 1)

    def backward_expert(m):
        def load_gates():
            gate_rows[...] = take_gates(m)

        (inner_grad,) = take_rows(
            m, 1, load_gates, lambda c: [matmul_t(rows_in[1, :, span(c)], wd[:, span(c)])]
        )
        inner_grad = inner_grad * gate_rows[...]
        gate_pre = gate_saved[m]
        sigmoid = 1.0 / (1.0 + jnp.exp(-gate_pre))
        pre_grad = (
            inner_grad * up_saved[m] * sigmoid * (1.0 + gate_pre * (1.0 - sigmoid))
        ).astype(bf16)
        up_grad = (inner_grad * gate_pre * sigmoid).astype(bf16)
        halves_and_combine(
            m, 1, lambda d: matmul_t(pre_grad, wg[span(d)]) + matmul_t(up_grad, wu[span(d)])
        )

    def score_slopes(m):
        upstream = grads[m].astype(f32)
        slopes = [
            jnp.sum(upstream * picked[m, k].astype(f32), axis=1, keepdims=True)
            for k in range(2)
        ]
        weighted = stats[m, 3] * slopes[0] + stats[m, 4] * slopes[1]
        total = stats[m, 1] + stats[m, 2]
        for k in range(2):
            chance = stats[m, 1 + k]
            stats[m, 5 + k] = (slopes[k] - weighted) / total * chance * (1.0 - chance)

    def backward_finish(m, c):
        if c == 0:
            score_slopes(m)
        named = expert_hot(m)
        router_table = (stats[m, 5] * named[0] + stats[m, 6] * named[1]).astype(bf16)
        routed = matmul(router_table, router_ref[:, span(c)])
        received = receive_combined(m, c, 1)
        tables = column_tables(m, c)
        summed = matmul(tables[0] + tables[1], received)
        inner = jnp.zeros((tokens, piece), f32)
        for q in range(CHUNK_PIECES[c]):
            at = slice(begin_of(c, q), begin_of(c, q + 1))
            near = slice(q * piece, (q + 1) * piece)
            normed_grad = summed[q * tokens : (q + 1) * tokens] + routed[:, near]
            normed_grad = normed_grad * gain_ref[:, at]
            inner += acts[m, :, at].astype(f32) * normed_grad
            kept[:, at] = normed_grad
        inner = jnp.sum(inner, axis=1, keepdims=True)
        if c > 0:
            inner += stats[m, 7]
        if c < CHUNKS - 1:
            stats[m, 7] = inner
            return
        scale = stats[m, 0]
        inner = scale * scale * scale * (inner / width)
        for d in range(CHUNKS):
            result = grads[m, :, span(d)].astype(f32) + scale * kept[:, span(d)]
            result -= acts[m, :, span(d)].astype(f32) * inner
            grad_ref[m, :, span(d)] = result.astype(bf16)

            @pl.when(section > 0)
            def _():
                pltpu.make_async_remote_copy(
                    src_ref=grad_ref.at[m, :, span(d)],
                    dst_ref=grads.at[m, :, span(d)],
                    send_sem=pipe_sem.at[1],
                    recv_sem=grad_sem.at[m * CHUNKS + d],
                    device_id={"pipe": section - 1},
                    device_id_type=MESH,
                ).start()

    steps = (
        forward_send,
        forward_expert,
        forward_finish,
        backward_send,
        backward_expert,
        backward_finish,
    )
    words = order_words(sections, micro_count)

    def run(i, carry):
        word, *counts = carry
        for w in range(len(words[0])):
            fresh = jnp.int32(0)
            for s, row in enumerate(words):
                fresh += jnp.where(section == s, row[w], 0)
            word = jnp.where(i == w * DIGITS, fresh, word)
        kind = lax.rem(word, 8)
        for number, step in enumerate(steps):
            if number in WHOLE:

                @pl.when(kind == number)
                def _():
                    step(counts[number])

                continue
            m, c = counts[number] // CHUNKS, lax.rem(counts[number], CHUNKS)
            for d in range(CHUNKS):

                @pl.when((kind == number) & (c == d))
                def _():
                    step(m, d)

        counts = [count + jnp.where(kind == n, 1, 0) for n, count in enumerate(counts)]
        return (word // 8, *counts)

    total_steps = micro_count * (4 * CHUNKS + 2)
    lax.fori_loop(0, total_steps, run, (jnp.int32(0),) * 7)

    @pl.when(section < sections - 1)
    def _():
        wait_all(out_ref, pipe_sem.at[0])

    @pl.when(section > 0)
    def _():
        wait_all(grad_ref, pipe_sem.at[1])


KINDS = "abcABC"
WHOLE = (1, 4)
DIGITS = 10
ORDERS = (
    "aaabcacabcacbccaabccAABAACBAACBCACACCBCC",
    "aabacacbaaccbccaabccAABCACABCAACBAACCBCC",
    "aabcacabaaccbcacAAaBbCCAAccBAACCBCAACBCC",
    "AAAAAaabBacacCAACbaaBccbCCBccaCaCAbBccCC",
)


def order_words(sections, micro_count):
    orders = ORDERS
    if (sections, micro_count) != (4, 4):
        orders = ("aabcc" * micro_count + "AABCC" * micro_count,) * (sections - 1)
        orders += ("AA" * micro_count + "aabcc" * micro_count + "BCC" * micro_count,)
    words = []
    for order in orders:
        row = []
        for begin in range(0, len(order), DIGITS):
            digits = [KINDS.index(kind) for kind in order[begin : begin + DIGITS]]
            row.append(sum(digit * 8**j for j, digit in enumerate(digits)))
        words.append(row)
    return words


def on_device(
    inputs, cotangent, norm_gain, router_weight, gate_weight, up_weight, down_weight, route_ids
):
    sections = lax.axis_size("pipe")
    chips = lax.axis_size("expert") // 2
    micro_count, tokens, width = inputs.shape
    experts = router_weight.shape[2]
    top_count = route_ids.shape[3]
    capacity = min(tokens, (5 * tokens * top_count + 4 * experts - 1) // (4 * experts))
    hidden = gate_weight.shape[2]
    piece = width // sum(CHUNK_PIECES)
    group = chips * capacity
    slots = -(-capacity // 8) * 8
    anywhere = pl.BlockSpec(memory_space=pl.ANY)
    inside = pl.BlockSpec(memory_space=pltpu.VMEM)
    bf16, f32 = jnp.bfloat16, jnp.float32
    out = jax.ShapeDtypeStruct((micro_count, tokens, width), bf16)
    dma = pltpu.SemaphoreType.DMA
    geometry = (sections, micro_count, chips, capacity)

    def per_chunk(shape_of, ways=0):
        chunks = tuple(pltpu.VMEM(shape_of(c), bf16) for c in range(CHUNKS))
        return (chunks, chunks) if ways else chunks

    def rows_of(c):
        return CHUNK_PIECES[c] * group // 2

    def blocks_of(c):
        return chips * block_rows(c, capacity) // 2

    def lanes_of(c):
        return CHUNK_PIECES[c] * tokens

    def exchange(c):
        return (micro_count, chips, block_rows(c, capacity), piece)

    def halves(c):
        return (CHUNK_PIECES[c], group, piece)

    def places(shape_of):
        return tuple(pltpu.VMEM(shape_of(c), jnp.int32) for c in range(CHUNKS))

    parts = micro_count * CHUNKS
    forward_out, backward_out = pl.pallas_call(
        functools.partial(relay_kernel, geometry),
        out_shape=(out, out),
        in_specs=[anywhere] * 2 + [inside] * 2 + [anywhere] * 3 + [inside],
        out_specs=(inside, inside),
        scratch_shapes=[
            pltpu.VMEM((width, hidden), bf16),
            pltpu.VMEM((width, hidden), bf16),
            pltpu.VMEM((hidden, width), bf16),
            pltpu.VMEM((micro_count, tokens, width), bf16),
            pltpu.VMEM((micro_count, tokens, width), bf16),
            per_chunk(lambda c: (rows_of(c), blocks_of(c))),
            per_chunk(lambda c: (blocks_of(c), rows_of(c))),
            pltpu.VMEM((group, chips * slots), bf16),
            places(lambda c: (micro_count, top_count, lanes_of(c))),
            places(lambda c: (micro_count, lanes_of(c), top_count)),
            pltpu.VMEM((micro_count, top_count, tokens), jnp.int32),
            per_chunk(exchange, 2),
            per_chunk(exchange, 2),
            per_chunk(exchange, 2),
            per_chunk(exchange, 2),
            per_chunk(exchange, 2),
            per_chunk(halves),
            per_chunk(halves),
            per_chunk(lambda c: (micro_count, *halves(c)), 2),
            pltpu.VMEM((micro_count, chips, slots, 128), f32),
            pltpu.VMEM((micro_count, 2, chips, slots, 128), f32),
            pltpu.VMEM((2, 2 * group, width), bf16),
            pltpu.VMEM((2 * group, 1), f32),
            pltpu.VMEM((micro_count, 2 * group, hidden), f32),
            pltpu.VMEM((micro_count, 2 * group, hidden), f32),
            pltpu.VMEM((2 * group, 1), f32),
            pltpu.VMEM((micro_count, top_count, tokens, width), bf16),
            pltpu.VMEM((tokens, width), f32),
            pltpu.VMEM((micro_count, 8, tokens, 1), f32),
            dma((3,)),
            dma((parts,)),
            dma((parts,)),
            dma((2,)),
            dma((2, parts)),
            dma((2, parts)),
            dma((CHUNKS,)),
            dma((2, parts)),
            dma((CHUNKS,)),
            dma((2, parts)),
            dma((2, parts)),
            dma((2, parts)),
            dma((micro_count, 2)),
            dma((micro_count, 2)),
        ],
        compiler_params=pltpu.CompilerParams(
            collective_id=0, has_side_effects=True, vmem_limit_bytes=66_000_000
        ),
    )(
        inputs,
        cotangent,
        norm_gain,
        router_weight[0].T,
        gate_weight[0],
        up_weight[0],
        down_weight[0],
        jnp.moveaxis(route_ids[0], 2, 1),
    )
    return (forward_out[None], backward_out[None])


def solution(mesh):
    return jax.shard_map(
        on_device,
        mesh=mesh,
        in_specs=(
            P(None, "expert", None),
            P(None, "expert", None),
            P("pipe", None),
            P("pipe", None, None),
            P("pipe", None, "expert"),
            P("pipe", None, "expert"),
            P("pipe", "expert", None),
            P("pipe", None, "expert", None),
        ),
        out_specs=(P("pipe", None, "expert", None), P("pipe", None, "expert", None)),
        check_vma=False,
    )
```

```python
import functools
import math

import jax
import jax.numpy as jnp
from jax import lax
from jax.experimental import pallas as pl
from jax.experimental.pallas import tpu as pltpu
from jax.sharding import PartitionSpec as P

EPSILON = 1e-06
CHUNK_PIECES = (8, 6)
CHUNKS = len(CHUNK_PIECES)
MESH = pl.DeviceIdType.MESH


def grid_of(chips):
    rows = math.isqrt(chips)
    while chips % rows:
        rows -= 1
    return rows, chips // rows


def block_rows(c, capacity):
    return -(-CHUNK_PIECES[c] * capacity // 8) * 8


def matmul(left, right):
    return jnp.dot(left, right, preferred_element_type=jnp.float32)


def matmul_t(left, right):
    return lax.dot_general(
        left, right, (((1,), (1,)), ((), ())), preferred_element_type=jnp.float32
    )


def relay_kernel(
    geometry,
    inputs_ref,
    cotangent_ref,
    gain_ref,
    router_ref,
    wg_hbm,
    wu_hbm,
    wd_hbm,
    ids_ref,
    out_ref,
    grad_ref,
    wg,
    wu,
    wd,
    acts,
    grads,
    unpack,
    repack,
    slot_pick,
    row_place,
    column_place,
    slot_place,
    dispatch_send,
    dispatch_recv,
    partner_rows,
    combine_send,
    combine_recv,
    half_send,
    half_own,
    half_recv,
    gate_send,
    gate_recv,
    rows_in,
    squares,
    gate_saved,
    up_saved,
    gate_rows,
    picked,
    kept,
    stats,
    weight_sem,
    act_sem,
    grad_sem,
    pipe_sem,
    dispatch_send_sem,
    dispatch_recv_sem,
    swap_send_sem,
    swap_recv_sem,
    half_send_sem,
    half_recv_sem,
    combine_send_sem,
    combine_recv_sem,
    gate_send_sem,
    gate_recv_sem,
):
    sections, micro_count, chips, capacity = geometry
    lines, columns = grid_of(chips)
    tokens, width = acts.shape[1], acts.shape[2]
    piece = width // sum(CHUNK_PIECES)
    group = chips * capacity
    half_group, half_chips = group // 2, chips // 2
    slots = gate_send.shape[2]
    hidden = wg.shape[1]
    experts = router_ref.shape[0]
    bf16, f32 = jnp.bfloat16, jnp.float32
    section = lax.axis_index("pipe")
    place = lax.axis_index("expert")
    core = lax.rem(place, 2)
    chip = place // 2
    line, column = chip // columns, lax.rem(chip, columns)
    partner = chip * 2 + (1 - core)
    others = pl.ds(1, chips - 1)

    def peer(step, sign, to_core=core):
        to_line = lax.rem(line + sign * (step // columns) + lines, lines)
        to_column = lax.rem(column + sign * lax.rem(step, columns) + columns, columns)
        return {"expert": (to_line * columns + to_column) * 2 + to_core}

    def begin_of(c, q=0):
        return (sum(CHUNK_PIECES[:c]) + q) * piece

    def span(c):
        return slice(begin_of(c), begin_of(c + 1))

    def pieces_of(value):
        return [value[:, q : q + piece] for q in range(0, value.shape[1], piece)]

    def block_of(c):
        return block_rows(c, capacity)

    barrier = pltpu.get_barrier_semaphore()

    def greet(step, carry):
        for to_core in (core, 1 - core):
            pl.semaphore_signal(
                barrier, inc=1, device_id=peer(step, 1, to_core), device_id_type=MESH
            )
        return carry

    weights = [
        pltpu.make_async_copy(source, target, weight_sem.at[i])
        for i, (source, target) in enumerate([(wg_hbm, wg), (wu_hbm, wu), (wd_hbm, wd)])
    ]

    def fetch(source, target, semaphore):
        for m in range(micro_count):
            for c in range(CHUNKS):
                pltpu.make_async_copy(
                    source.at[m, :, span(c)],
                    target.at[m, :, span(c)],
                    semaphore.at[m * CHUNKS + c],
                ).start()

    @pl.when(section == 0)
    def _():
        fetch(inputs_ref, acts, act_sem)

    @pl.when(section == sections - 1)
    def _():
        fetch(cotangent_ref, grads, grad_sem)

    for copy in weights:
        copy.start()
    lax.fori_loop(1, chips, greet, 0)
    pl.semaphore_signal(barrier, inc=1, device_id={"expert": partner}, device_id_type=MESH)
    for sign in (1, sections - 1):
        pl.semaphore_signal(
            barrier,
            inc=1,
            device_id={"pipe": lax.rem(section + sign, sections)},
            device_id_type=MESH,
        )

    def iota(shape, axis):
        return lax.broadcasted_iota(jnp.int32, shape, axis)

    def hot(condition):
        return jnp.where(condition, 1.0, 0.0).astype(bf16)

    earlier = hot(iota((tokens, tokens), 0) < iota((tokens, tokens), 1))
    for m in range(micro_count):
        ids = ids_ref[m]
        found = [hot(iota((experts, tokens), 0) == ids[k : k + 1]) for k in range(2)]
        counts = matmul(found[0] + found[1], earlier)
        ranks = [
            jnp.sum(counts * found[k].astype(f32), axis=0, keepdims=True) for k in range(2)
        ]
        ranks = jnp.concatenate(ranks, axis=0)
        to_line = lax.rem(ids // columns - line + lines, lines)
        to_column = lax.rem(lax.rem(ids, columns) - column + columns, columns)
        steps_to = (to_line * columns + to_column).astype(f32).astype(bf16)
        ranks_to = ranks.astype(bf16)
        for c in range(CHUNKS):
            lanes = CHUNK_PIECES[c] * tokens
            across = hot(iota((tokens, lanes), 0) == lax.rem(iota((1, lanes), 1), tokens))
            down = hot(lax.rem(iota((lanes, 1), 0), tokens) == iota((lanes, tokens), 1))
            where = matmul(steps_to, across).astype(jnp.int32) * block_of(c)
            where += matmul(ranks_to, across).astype(jnp.int32)
            row_place[c][m] = where + (iota((1, lanes), 1) // tokens) * capacity
            where = matmul_t(down, steps_to).astype(jnp.int32) * block_of(c)
            where += matmul_t(down, ranks_to).astype(jnp.int32)
            column_place[c][m] = where + (iota((lanes, 1), 0) // tokens) * capacity
        slot_place[m] = (steps_to.astype(f32) * slots + ranks).astype(jnp.int32)

    pl.semaphore_wait(barrier, 2 * (chips - 1) + 1 + 2)

    def build_matrices():
        for c in range(CHUNKS):

            def place_of(number):
                within = lax.rem(number, block_of(c))
                q = within // capacity
                row = q * half_group + (number // block_of(c)) * capacity + lax.rem(within, capacity)
                return jnp.where(within < CHUNK_PIECES[c] * capacity, row, -1)

            shape = (CHUNK_PIECES[c] * half_group, half_chips * block_of(c))
            unpack[c][...] = hot(iota(shape, 0) == place_of(iota((1, shape[1]), 1)))
            repack[c][...] = hot(iota(shape[::-1], 1) == place_of(iota((shape[1], 1), 0)))
        shape = (group, chips * slots)
        wanted = iota((group, 1), 0)
        wanted = (wanted // capacity) * slots + lax.rem(wanted, capacity)
        slot_pick[...] = hot(iota(shape, 1) == wanted)

    def wait_all(buffer, semaphore):
        pltpu.make_async_copy(buffer, buffer, semaphore).wait()

    def post(values, m, c, send, recv, send_sem, recv_sem, sign):
        values = values.astype(bf16).reshape(chips, block_of(c), piece)
        recv[m, 0] = values[0]
        send[m, others] = values[1:]

        def start(step, carry):
            pltpu.make_async_remote_copy(
                src_ref=send.at[m, step],
                dst_ref=recv.at[m, step],
                send_sem=send_sem.at[m * CHUNKS + c],
                recv_sem=recv_sem.at[m * CHUNKS + c],
                device_id=peer(step, sign),
                device_id_type=MESH,
            ).start()
            return carry

        lax.fori_loop(1, chips, start, 0)

    def dispatch(stacked, m, c, way):
        target = row_place[c][m]
        rows = iota((chips * block_of(c), target.shape[1]), 0)
        table = hot(rows == target[0:1]) + hot(rows == target[1:2])
        post(
            matmul(table, stacked),
            m,
            c,
            dispatch_send[way][c],
            dispatch_recv[way][c],
            dispatch_send_sem.at[way],
            dispatch_recv_sem.at[way],
            1,
        )

    def expert_hot(m):
        same = hot(iota((tokens, tokens), 0) == iota((tokens, tokens), 1))
        names = matmul_t(same, ids_ref[m].astype(f32).astype(bf16)).astype(jnp.int32)
        return [
            jnp.where(iota((tokens, experts), 1) == names[:, k : k + 1], 1.0, 0.0)
            for k in range(2)
        ]

    def unpack_rows(source, m, c, way, part):
        rows = [
            matmul(unpack[c][...], blocks.reshape(half_chips * block_of(c), piece))
            for blocks in (source[m, :half_chips], source[m, half_chips:])
        ]
        mine = slice(part * group, (part + 1) * group)
        square = jnp.zeros((group, piece), f32)
        for q in range(CHUNK_PIECES[c]):
            at = slice(begin_of(c, q), begin_of(c, q + 1))
            found = [half[q * half_group : (q + 1) * half_group] for half in rows]
            found = jnp.concatenate(found, axis=0)
            if way == 0:
                square += found * found
                found = found * gain_ref[:, at]
            rows_in[way, mine, at] = found.astype(bf16)
        if way == 0:
            square = jnp.sum(square, axis=1, keepdims=True)
            squares[mine] = square if c == 0 else squares[mine] + square

    def take_rows(m, way, meanwhile, product):
        swaps = []
        for c in range(CHUNKS):
            number = m * CHUNKS + c
            send, recv = dispatch_send[way][c], dispatch_recv[way][c]
            wait_all(recv.at[m, others], dispatch_recv_sem.at[way, number])
            swap = pltpu.make_async_remote_copy(
                src_ref=recv.at[m],
                dst_ref=partner_rows[way][c].at[m],
                send_sem=swap_send_sem.at[c],
                recv_sem=swap_recv_sem.at[way, number],
                device_id={"expert": partner},
                device_id_type=MESH,
            )
            swap.start()
            swaps.append(swap)
            wait_all(send.at[m, others], dispatch_send_sem.at[way, number])
            unpack_rows(recv, m, c, way, 0)
        meanwhile()
        total = None
        for c in range(CHUNKS):
            swaps[c].wait()
            unpack_rows(partner_rows[way][c], m, c, way, 1)
            found = product(c)
            total = found if total is None else [a + b for a, b in zip(total, found)]
        return total

    def halves_and_combine(m, way, product):
        copies = []
        for c in range(CHUNKS):
            part = product(c).astype(bf16)
            for q, values in enumerate(pieces_of(part)):
                half_own[c][q] = values[:group]
                half_send[c][q] = values[group:]
            copy = pltpu.make_async_remote_copy(
                src_ref=half_send[c],
                dst_ref=half_recv[way][c].at[m],
                send_sem=half_send_sem.at[c],
                recv_sem=half_recv_sem.at[way, m * CHUNKS + c],
                device_id={"expert": partner},
                device_id_type=MESH,
            )
            copy.start()
            copies.append(copy)
        for c in range(CHUNKS):
            copies[c].wait()
            total = half_own[c][...].astype(f32) + half_recv[way][c][m].astype(f32)
            packed = [
                matmul(
                    repack[c][...],
                    half.reshape(CHUNK_PIECES[c] * half_group, piece).astype(bf16),
                )
                for half in (total[:, :half_group], total[:, half_group:])
            ]
            post(
                jnp.concatenate(packed, axis=0),
                m,
                c,
                combine_send[way][c],
                combine_recv[way][c],
                combine_send_sem.at[way],
                combine_recv_sem.at[way],
                -1,
            )

    def send_gates(m, gates):
        target = slot_place[m]
        rows = iota((chips * slots, tokens), 0)
        tables = [hot(rows == target[k : k + 1]) for k in range(2)]
        spread = jnp.zeros((chips * slots, 128), f32)
        for k in range(2):
            value = jnp.broadcast_to(gates[k], (tokens, 128))
            high = value.astype(bf16)
            low = (value - high.astype(f32)).astype(bf16)
            spread += matmul(tables[k], high) + matmul(tables[k], low)
        spread = spread.reshape(chips, slots, 128)
        gate_send[m] = spread
        gate_recv[m, 0, 0] = spread[0]

        def copy_to(step, part):
            pltpu.make_async_remote_copy(
                src_ref=gate_send.at[m, step],
                dst_ref=gate_recv.at[m, part, step],
                send_sem=gate_send_sem.at[m, part],
                recv_sem=gate_recv_sem.at[m, part],
                device_id=peer(step, 1, core if part == 0 else 1 - core),
                device_id_type=MESH,
            ).start()

        def start(step, carry):
            copy_to(step, 0)
            copy_to(step, 1)
            return carry

        copy_to(0, 1)
        lax.fori_loop(1, chips, start, 0)

    def take_gates(m):
        gates = []
        for part, arrived in enumerate((others, pl.ds(0, chips))):
            wait_all(gate_recv.at[m, part, arrived], gate_recv_sem.at[m, part])
            wait_all(gate_send.at[m, arrived], gate_send_sem.at[m, part])
            value = gate_recv[m, part].reshape(chips * slots, 128)
            high = value.astype(bf16)
            low = (value - high.astype(f32)).astype(bf16)
            gates.append(matmul(slot_pick[...], high) + matmul(slot_pick[...], low))
        return jnp.concatenate(gates, axis=0)[:, :1]

    def forward_send(m, c):
        wait_all(acts.at[m, :, span(c)], act_sem.at[m * CHUNKS + c])
        dispatch(jnp.concatenate(pieces_of(acts[m, :, span(c)]), axis=0), m, c, 0)
        if c < CHUNKS - 1:
            return
        wide_in = acts[m].astype(f32)
        scale = lax.rsqrt(jnp.mean(wide_in * wide_in, axis=1, keepdims=True) + EPSILON)
        normed = (wide_in * scale * gain_ref[...]).astype(bf16)
        logits = matmul_t(normed, router_ref[...])
        chances = [
            1.0 / (1.0 + jnp.exp(-jnp.sum(logits * named, axis=1, keepdims=True)))
            for named in expert_hot(m)
        ]
        total = chances[0] + chances[1]
        gates = [chance / total for chance in chances]
        send_gates(m, gates)
        stats[m, 0] = scale
        for k in range(2):
            stats[m, 1 + k] = chances[k]
            stats[m, 3 + k] = gates[k]

    def forward_expert(m):
        @pl.when(m == 0)
        def _():
            build_matrices()
            for copy in weights:
                copy.wait()

        def product(c):
            rows = rows_in[0, :, span(c)]
            return [matmul(rows, wg[span(c)]), matmul(rows, wu[span(c)])]

        gate_pre, up_pre = take_rows(m, 0, lambda: None, product)
        scale = lax.rsqrt(squares[...] / width + EPSILON)
        gate_pre = gate_pre * scale
        up_pre = up_pre * scale
        gate_saved[m] = gate_pre
        up_saved[m] = up_pre
        inner = (gate_pre / (1.0 + jnp.exp(-gate_pre)) * up_pre).astype(bf16)
        halves_and_combine(m, 0, lambda d: matmul(inner, wd[:, span(d)]))

    def receive_combined(m, c, way):
        number = m * CHUNKS + c
        recv = combine_recv[way][c]
        wait_all(recv.at[m, others], combine_recv_sem.at[way, number])
        wait_all(combine_send[way][c].at[m, others], combine_send_sem.at[way, number])
        return recv[m].reshape(chips * block_of(c), piece)

    def column_tables(m, c):
        target = column_place[c][m]
        places = iota((target.shape[0], chips * block_of(c)), 1)
        return [hot(places == target[:, k : k + 1]) for k in range(2)]

    def forward_finish(m, c):
        received = receive_combined(m, c, 0)
        found = [matmul(table, received) for table in column_tables(m, c)]
        for q in range(CHUNK_PIECES[c]):
            at = slice(begin_of(c, q), begin_of(c, q + 1))
            total = acts[m, :, at].astype(f32)
            for k in range(2):
                rows = found[k][q * tokens : (q + 1) * tokens]
                picked[m, k, :, at] = rows.astype(bf16)
                total += stats[m, 3 + k] * rows
            out_ref[m, :, at] = total.astype(bf16)

        @pl.when(section < sections - 1)
        def _():
            pltpu.make_async_remote_copy(
                src_ref=out_ref.at[m, :, span(c)],
                dst_ref=acts.at[m, :, span(c)],
                send_sem=pipe_sem.at[0],
                recv_sem=act_sem.at[m * CHUNKS + c],
                device_id={"pipe": section + 1},
                device_id_type=MESH,
            ).start()

    def backward_send(m, c):
        wait_all(grads.at[m, :, span(c)], grad_sem.at[m * CHUNKS + c])
        dispatch(jnp.concatenate(pieces_of(grads[m, :, span(c)]), axis=0), m, c, 1)

    def backward_expert(m):
        def load_gates():
            gate_rows[...] = take_gates(m)

        (inner_grad,) = take_rows(
            m, 1, load_gates, lambda c: [matmul_t(rows_in[1, :, span(c)], wd[:, span(c)])]
        )
        inner_grad = inner_grad * gate_rows[...]
        gate_pre = gate_saved[m]
        sigmoid = 1.0 / (1.0 + jnp.exp(-gate_pre))
        pre_grad = (
            inner_grad * up_saved[m] * sigmoid * (1.0 + gate_pre * (1.0 - sigmoid))
        ).astype(bf16)
        up_grad = (inner_grad * gate_pre * sigmoid).astype(bf16)
        halves_and_combine(
            m, 1, lambda d: matmul_t(pre_grad, wg[span(d)]) + matmul_t(up_grad, wu[span(d)])
        )

    def score_slopes(m):
        upstream = grads[m].astype(f32)
        slopes = [
            jnp.sum(upstream * picked[m, k].astype(f32), axis=1, keepdims=True)
            for k in range(2)
        ]
        weighted = stats[m, 3] * slopes[0] + stats[m, 4] * slopes[1]
        total = stats[m, 1] + stats[m, 2]
        for k in range(2):
            chance = stats[m, 1 + k]
            stats[m, 5 + k] = (slopes[k] - weighted) / total * chance * (1.0 - chance)

    def backward_finish(m, c):
        if c == 0:
            score_slopes(m)
        named = expert_hot(m)
        router_table = (stats[m, 5] * named[0] + stats[m, 6] * named[1]).astype(bf16)
        routed = matmul(router_table, router_ref[:, span(c)])
        received = receive_combined(m, c, 1)
        tables = column_tables(m, c)
        summed = matmul(tables[0] + tables[1], received)
        inner = jnp.zeros((tokens, piece), f32)
        for q in range(CHUNK_PIECES[c]):
            at = slice(begin_of(c, q), begin_of(c, q + 1))
            near = slice(q * piece, (q + 1) * piece)
            normed_grad = summed[q * tokens : (q + 1) * tokens] + routed[:, near]
            normed_grad = normed_grad * gain_ref[:, at]
            inner += acts[m, :, at].astype(f32) * normed_grad
            kept[:, at] = normed_grad
        inner = jnp.sum(inner, axis=1, keepdims=True)
        if c > 0:
            inner += stats[m, 7]
        if c < CHUNKS - 1:
            stats[m, 7] = inner
            return
        scale = stats[m, 0]
        inner = scale * scale * scale * (inner / width)
        for d in range(CHUNKS):
            result = grads[m, :, span(d)].astype(f32) + scale * kept[:, span(d)]
            result -= acts[m, :, span(d)].astype(f32) * inner
            grad_ref[m, :, span(d)] = result.astype(bf16)

            @pl.when(section > 0)
            def _():
                pltpu.make_async_remote_copy(
                    src_ref=grad_ref.at[m, :, span(d)],
                    dst_ref=grads.at[m, :, span(d)],
                    send_sem=pipe_sem.at[1],
                    recv_sem=grad_sem.at[m * CHUNKS + d],
                    device_id={"pipe": section - 1},
                    device_id_type=MESH,
                ).start()

    steps = (
        forward_send,
        forward_expert,
        forward_finish,
        backward_send,
        backward_expert,
        backward_finish,
    )
    words = order_words(sections, micro_count)

    def run(i, carry):
        word, *counts = carry
        for w in range(len(words[0])):
            fresh = jnp.int32(0)
            for s, row in enumerate(words):
                fresh += jnp.where(section == s, row[w], 0)
            word = jnp.where(i == w * DIGITS, fresh, word)
        kind = lax.rem(word, 8)
        for number, step in enumerate(steps):
            if number in WHOLE:

                @pl.when(kind == number)
                def _():
                    step(counts[number])

                continue
            m, c = counts[number] // CHUNKS, lax.rem(counts[number], CHUNKS)
            for d in range(CHUNKS):

                @pl.when((kind == number) & (c == d))
                def _():
                    step(m, d)

        counts = [count + jnp.where(kind == n, 1, 0) for n, count in enumerate(counts)]
        return (word // 8, *counts)

    total_steps = micro_count * (4 * CHUNKS + 2)
    lax.fori_loop(0, total_steps, run, (jnp.int32(0),) * 7)

    @pl.when(section < sections - 1)
    def _():
        wait_all(out_ref, pipe_sem.at[0])

    @pl.when(section > 0)
    def _():
        wait_all(grad_ref, pipe_sem.at[1])


KINDS = "abcABC"
WHOLE = (1, 4)
DIGITS = 10
ORDERS = (
    "aaabcacabcacbccaabccAABAACBAACBCACACCBCC",
    "aabacacbaaccbccaabccAABCACABCAACBAACCBCC",
    "aabcacabaaccbcacAAaBbCCAAccBAACCBCAACBCC",
    "AAAAAaabBacacCAACbaaBccbCCBccaCaCAbBccCC",
)


def order_words(sections, micro_count):
    orders = ORDERS
    if (sections, micro_count) != (4, 4):
        orders = ("aabcc" * micro_count + "AABCC" * micro_count,) * (sections - 1)
        orders += ("AA" * micro_count + "aabcc" * micro_count + "BCC" * micro_count,)
    words = []
    for order in orders:
        row = []
        for begin in range(0, len(order), DIGITS):
            digits = [KINDS.index(kind) for kind in order[begin : begin + DIGITS]]
            row.append(sum(digit * 8**j for j, digit in enumerate(digits)))
        words.append(row)
    return words


def on_device(
    inputs, cotangent, norm_gain, router_weight, gate_weight, up_weight, down_weight, route_ids
):
    sections = lax.axis_size("pipe")
    chips = lax.axis_size("expert") // 2
    micro_count, tokens, width = inputs.shape
    experts = router_weight.shape[2]
    top_count = route_ids.shape[3]
    capacity = min(tokens, (5 * tokens * top_count + 4 * experts - 1) // (4 * experts))
    hidden = gate_weight.shape[2]
    piece = width // sum(CHUNK_PIECES)
    group = chips * capacity
    slots = -(-capacity // 8) * 8
    anywhere = pl.BlockSpec(memory_space=pl.ANY)
    inside = pl.BlockSpec(memory_space=pltpu.VMEM)
    bf16, f32 = jnp.bfloat16, jnp.float32
    out = jax.ShapeDtypeStruct((micro_count, tokens, width), bf16)
    dma = pltpu.SemaphoreType.DMA
    geometry = (sections, micro_count, chips, capacity)

    def per_chunk(shape_of, ways=0):
        chunks = tuple(pltpu.VMEM(shape_of(c), bf16) for c in range(CHUNKS))
        return (chunks, chunks) if ways else chunks

    def rows_of(c):
        return CHUNK_PIECES[c] * group // 2

    def blocks_of(c):
        return chips * block_rows(c, capacity) // 2

    def lanes_of(c):
        return CHUNK_PIECES[c] * tokens

    def exchange(c):
        return (micro_count, chips, block_rows(c, capacity), piece)

    def halves(c):
        return (CHUNK_PIECES[c], group, piece)

    def places(shape_of):
        return tuple(pltpu.VMEM(shape_of(c), jnp.int32) for c in range(CHUNKS))

    parts = micro_count * CHUNKS
    forward_out, backward_out = pl.pallas_call(
        functools.partial(relay_kernel, geometry),
        out_shape=(pltpu.VMEM(out.shape, bf16),) * 2,
        in_specs=[anywhere] * 2 + [inside] * 2 + [anywhere] * 3 + [inside],
        out_specs=(inside, inside),
        scratch_shapes=[
            pltpu.VMEM((width, hidden), bf16),
            pltpu.VMEM((width, hidden), bf16),
            pltpu.VMEM((hidden, width), bf16),
            pltpu.VMEM((micro_count, tokens, width), bf16),
            pltpu.VMEM((micro_count, tokens, width), bf16),
            per_chunk(lambda c: (rows_of(c), blocks_of(c))),
            per_chunk(lambda c: (blocks_of(c), rows_of(c))),
            pltpu.VMEM((group, chips * slots), bf16),
            places(lambda c: (micro_count, top_count, lanes_of(c))),
            places(lambda c: (micro_count, lanes_of(c), top_count)),
            pltpu.VMEM((micro_count, top_count, tokens), jnp.int32),
            per_chunk(exchange, 2),
            per_chunk(exchange, 2),
            per_chunk(exchange, 2),
            per_chunk(exchange, 2),
            per_chunk(exchange, 2),
            per_chunk(halves),
            per_chunk(halves),
            per_chunk(lambda c: (micro_count, *halves(c)), 2),
            pltpu.VMEM((micro_count, chips, slots, 128), f32),
            pltpu.VMEM((micro_count, 2, chips, slots, 128), f32),
            pltpu.VMEM((2, 2 * group, width), bf16),
            pltpu.VMEM((2 * group, 1), f32),
            pltpu.VMEM((micro_count, 2 * group, hidden), f32),
            pltpu.VMEM((micro_count, 2 * group, hidden), f32),
            pltpu.VMEM((2 * group, 1), f32),
            pltpu.VMEM((micro_count, top_count, tokens, width), bf16),
            pltpu.VMEM((tokens, width), f32),
            pltpu.VMEM((micro_count, 8, tokens, 1), f32),
            dma((3,)),
            dma((parts,)),
            dma((parts,)),
            dma((2,)),
            dma((2, parts)),
            dma((2, parts)),
            dma((CHUNKS,)),
            dma((2, parts)),
            dma((CHUNKS,)),
            dma((2, parts)),
            dma((2, parts)),
            dma((2, parts)),
            dma((micro_count, 2)),
            dma((micro_count, 2)),
        ],
        compiler_params=pltpu.CompilerParams(
            collective_id=0, has_side_effects=True, vmem_limit_bytes=62_500_000
        ),
    )(
        inputs,
        cotangent,
        norm_gain,
        router_weight[0].T,
        gate_weight[0],
        up_weight[0],
        down_weight[0],
        jnp.moveaxis(route_ids[0], 2, 1),
    )
    return (forward_out[None], backward_out[None])


def solution(mesh):
    return jax.shard_map(
        on_device,
        mesh=mesh,
        in_specs=(
            P(None, "expert", None),
            P(None, "expert", None),
            P("pipe", None),
            P("pipe", None, None),
            P("pipe", None, "expert"),
            P("pipe", None, "expert"),
            P("pipe", "expert", None),
            P("pipe", None, "expert", None),
        ),
        out_specs=(P("pipe", None, "expert", None), P("pipe", None, "expert", None)),
        check_vma=False,
    )
```
